32 devices in a mesh: ha: 4 (over z), wa: 8 (over y, x, core).
Axes of the slice: x: 2, y: 2, z: 4, core: 2. Of those that a mesh axis runs over, the one named last changes fastest.
Arguments:
- tokens: bfloat16 [32, 128, 512], P('ha', 'wa'), may hold values from -6 to 6
- cotangent: bfloat16 [32, 128, 512], P('ha', 'wa'), may hold values from -6 to 6
- state_in: float32 [32, 128, 16], P('ha', 'wa'), may hold values from -0.25 to 0.25
- state_out: float32 [32, 128, 16], P('ha', 'wa'), may hold values from -0.25 to 0.25
- width_decay: float32 [32, 128, 8], P('ha', 'wa'), may hold values from -1.6 to 0
- height_decay: float32 [32, 128, 8], P('ha', 'wa'), may hold values from -1.6 to 0
Outputs:
- tokens_grad: float32 [32, 128, 512], P('ha', 'wa')
- state_in_grad: float32 [32, 128, 16], P('ha', 'wa')
- state_out_grad: float32 [32, 128, 16], P('ha', 'wa')
- width_decay_grad: float32 [32, 128, 8], P('ha', 'wa')
- height_decay_grad: float32 [32, 128, 8], P('ha', 'wa')
The draws below stay inside these ranges and needn't reach their ends.
All inputs are finite; a program needn't handle non-finite values.
Results may differ from the reference program's by a relative error of at most 0.0003.
Values sent between devices are 32-bit elements; how exact they have to be, the bound alone decides.
A program may use at most 128 MiB of HBM per device.

```python
import jax
import jax.numpy as jnp
from jax import lax

D = 512
G = 8
N = 16
HEIGHT = 32
WIDTH = 128


def decay_logs(key, direction, sequence_length):
    key_list = jax.random.split(key, 7)
    fast_count = jax.random.randint(key_list[0], (), 2, 5)
    ranking = jax.random.permutation(key_list[1], G)
    is_fast = ranking < fast_count
    slow_rate = jax.random.uniform(key_list[2], (G,), jnp.float32, 0.1, 0.5) / sequence_length
    fast_rate = jnp.exp(jax.random.uniform(key_list[3], (G,), jnp.float32, jnp.log(1.0 / 50.0), jnp.log(1.0 / 30.0)))
    cluster_decay_rate = jnp.where(is_fast, fast_rate, slow_rate)
    texture_jitter = jnp.exp(jax.random.uniform(key_list[4], (HEIGHT, WIDTH, G), jnp.float32, jnp.log(0.5), jnp.log(2.0)))
    position_indices = jax.random.randint(key_list[5], (3,), 0, sequence_length)
    loss_values = jax.random.uniform(key_list[6], (3,), jnp.float32, 0.22, 0.51)
    spike_stripe_row = jnp.sum(loss_values[:, None] * (jnp.arange(sequence_length)[None, :] == position_indices[:, None]).astype(jnp.float32), axis=0)
    if direction == 1:
        spike_lattice = spike_stripe_row[None, :, None]
    else:
        spike_lattice = spike_stripe_row[:, None, None]
    return (-(cluster_decay_rate * texture_jitter + spike_lattice)).astype(jnp.float32)


def draw_width_decay(key, part):
    return decay_logs(jax.random.fold_in(key, 11), 1, WIDTH)


def draw_height_decay(key, part):
    return decay_logs(jax.random.fold_in(key, 23), 0, HEIGHT)


def steps_of(rng, shape, cuts, least, high):
    loudness = 1.0
    for axis_at, blocks in cuts:
        draws = jax.random.uniform(jax.random.fold_in(jax.random.fold_in(rng, 6), axis_at), (blocks,), jnp.float32, least / len(cuts), high / len(cuts))
        loudness = loudness * jnp.repeat(jnp.exp(draws), shape[axis_at] // blocks).reshape((-1,) + (1,) * (len(shape) - 1 - axis_at))
    return loudness


def centred(own_key, extent, scale, bound, cuts=(), kind=jnp.bfloat16):
    level = steps_of(own_key, extent, cuts, -0.22, 0.18) if cuts else 1.0
    entries = jax.random.normal(own_key, extent, jnp.float32) * scale * level
    return jnp.minimum(jnp.maximum(entries, -bound), bound).astype(kind)


def setup_inputs(seed: int = 0) -> dict:
    key_of = jax.random.split(jax.random.key(seed), 7)
    return {
        "tokens": centred(key_of[0], (HEIGHT, WIDTH, D), 1.0, 6.0, ((0, 4), (1, 8))),
        "cotangent": centred(key_of[1], (HEIGHT, WIDTH, D), 1.0, 6.0, ((0, 4), (1, 8))),
        "state_in": centred(key_of[2], (HEIGHT, WIDTH, N), 0.03125, 0.25, ((0, 4), (1, 8)), jnp.float32),
        "state_out": centred(key_of[3], (HEIGHT, WIDTH, N), 0.03125, 0.25, ((0, 4), (1, 8)), jnp.float32),
        "width_decay": draw_width_decay(jax.random.fold_in(key_of[6], 71), 0),
        "height_decay": draw_height_decay(jax.random.fold_in(key_of[6], 71), 0),
    }


def advance(carry, item):
    rate, term = item
    carry = rate * carry + term
    return carry, carry


def retreat(carry, item):
    rate, term = item
    total = term + carry
    return rate * total, total


def slab_grads(values, grads_out, log_width, log_height, state_in, state_out):
    width_rate = jnp.exp(log_width)[:, :, None, :]
    height_rate = jnp.exp(log_height)[:, :, None, :]
    slab_width = values.shape[2]
    driven = state_in[:, :, :, None] * values[:, :, None, :]
    zero_rows = jnp.zeros((HEIGHT, N, slab_width), jnp.float32)
    zero_cols = jnp.zeros((WIDTH, N, slab_width), jnp.float32)
    ignored, states = lax.scan(advance, zero_rows, (jnp.swapaxes(width_rate, 0, 1), jnp.swapaxes(driven, 0, 1)))
    states = jnp.swapaxes(states, 0, 1)
    ignored, totals = lax.scan(advance, zero_cols, (height_rate, states))
    seeded = state_out[:, :, :, None] * grads_out[:, :, None, :]
    ignored, col_grad = lax.scan(retreat, zero_cols, (height_rate, seeded), reverse=True)
    earlier_rows = jnp.concatenate([jnp.zeros_like(totals[:1]), totals[:-1]], axis=0)
    height_grad = jnp.exp(log_height) * jnp.sum(col_grad * earlier_rows, axis=2)
    out_grad = jnp.sum(totals * grads_out[:, :, None, :], axis=3)
    ignored, row_grad = lax.scan(retreat, zero_rows, (jnp.swapaxes(width_rate, 0, 1), jnp.swapaxes(col_grad, 0, 1)), reverse=True)
    row_grad = jnp.swapaxes(row_grad, 0, 1)
    earlier_cols = jnp.concatenate([jnp.zeros_like(states[:, :1]), states[:, :-1]], axis=1)
    width_grad = jnp.exp(log_width) * jnp.sum(row_grad * earlier_cols, axis=2)
    in_grad = jnp.sum(row_grad * values[:, :, None, :], axis=3)
    token_grad = jnp.sum(row_grad * state_in[:, :, :, None], axis=2)
    return token_grad, in_grad, out_grad, width_grad, height_grad


def reference(tokens, cotangent, state_in, state_out, width_decay, height_decay):
    slab_width = 8
    count = D // slab_width
    group_width = D // G

    def one_slab(carry, number):
        offset = (number * slab_width).astype(jnp.int32)
        values = lax.dynamic_slice_in_dim(tokens, offset, slab_width, 2).astype(jnp.float32)
        grads_out = lax.dynamic_slice_in_dim(cotangent, offset, slab_width, 2).astype(jnp.float32)
        group = (offset // group_width).astype(jnp.int32)
        log_width = jnp.broadcast_to(lax.dynamic_slice_in_dim(width_decay, group, 1, 2), (HEIGHT, WIDTH, slab_width))
        log_height = jnp.broadcast_to(lax.dynamic_slice_in_dim(height_decay, group, 1, 2), (HEIGHT, WIDTH, slab_width))
        token_grad, in_grad, out_grad, width_grad, height_grad = slab_grads(values, grads_out, log_width, log_height, state_in, state_out)
        return (carry[0] + in_grad, carry[1] + out_grad), (token_grad, jnp.sum(width_grad, axis=2), jnp.sum(height_grad, axis=2))

    start = (jnp.zeros((HEIGHT, WIDTH, N), jnp.float32), jnp.zeros((HEIGHT, WIDTH, N), jnp.float32))
    sums, slabs = lax.scan(one_slab, start, jnp.arange(count, dtype=jnp.int32))
    token_parts, width_parts, height_parts = slabs
    tokens_grad = jnp.transpose(token_parts, (1, 2, 0, 3)).reshape(HEIGHT, WIDTH, D)
    width_decay_grad = jnp.transpose(jnp.sum(width_parts.reshape(G, group_width // slab_width, HEIGHT, WIDTH), axis=1), (1, 2, 0))
    height_decay_grad = jnp.transpose(jnp.sum(height_parts.reshape(G, group_width // slab_width, HEIGHT, WIDTH), axis=1), (1, 2, 0))
    return tokens_grad, sums[0], sums[1], width_decay_grad, height_decay_grad
```

```python
import functools

import jax
import jax.numpy as jnp
from jax import lax
from jax.experimental import pallas as pl
from jax.experimental.pallas import tpu as pltpu
from jax.sharding import PartitionSpec as P

MESH = pl.DeviceIdType.MESH
F32 = jnp.float32
BF16 = jnp.bfloat16
HIGHEST = lax.Precision.HIGHEST


def swap(v):
    half = v.shape[-1] // 2
    if v.shape[-1] % 128 == 0:
        return pltpu.roll(v, half, v.ndim - 1)
    return jnp.concatenate([v[..., half:], v[..., :half]], axis=-1)


def low(shape):
    return lax.broadcasted_iota(jnp.int32, shape, len(shape) - 1) < shape[-1] // 2


def cross(a, b):
    keep = low(a.shape)
    return jnp.where(keep, a, swap(b)), jnp.where(keep, swap(a), b)


def exchange(
    ha,
    chips,
    pair,
    tok_in,
    cot_in,
    b_in,
    c_in,
    wl,
    hl,
    tok_home,
    in_home,
    fin_home,
    msg_c,
    msg_x,
    land_c,
    land_x,
    small,
    cot,
    x,
    wr,
    hr,
    cb,
    bb,
    grads,
    rows_grad,
    hold,
    total,
    ends_b,
    ends_f,
    cin_b,
    cin_f,
    pw,
    pc_msg,
    pc_land,
    wb_msg,
    wb_land,
    wf_msg,
    wf_land,
    place,
    prod_b,
    prod_f,
    tok_rows,
    tok_msg,
    in_msg,
    fin_msg,
    s_small,
    r_small,
    s_core,
    r_core,
    s_in,
    r_in,
    s_pc,
    r_pc,
    s_wide,
    r_wide,
    s_out,
    r_out,
):
    rows, cols, channels = tok_in.shape
    n = b_in.shape[2]
    groups = wl.shape[1]
    lanes = channels // ha
    share = lanes // pair
    owners = ha * pair
    high = ha * rows
    tokens = rows * cols
    me_z = lax.axis_index("ha")
    me_w = lax.axis_index("wa")
    chip = me_w // pair
    core = lax.rem(me_w, pair)
    me_q = me_z * pair + core
    mine = lax.div(me_q * share, channels // groups)

    def column(q):
        return {"ha": lax.div(q, pair), "wa": chip * pair + lax.rem(q, pair)}

    def across(c):
        return {"wa": c * pair + core}

    def remote(src, dst, ss, rs, device):
        return pltpu.make_async_remote_copy(
            src_ref=src, dst_ref=dst, send_sem=ss, recv_sem=rs, device_id=device, device_id_type=MESH
        )

    def dot(a, b, dims):
        return lax.dot_general(a, b, (dims, ((), ())), precision=HIGHEST, preferred_element_type=F32)

    barrier = pltpu.get_barrier_semaphore()
    for d in range(1, owners):
        pl.semaphore_signal(
            barrier, inc=1, device_id=column(lax.rem(me_q + d, owners)), device_id_type=MESH
        )
    for d in range(1, chips):
        pl.semaphore_signal(
            barrier, inc=1, device_id=across(lax.rem(chip + d, chips)), device_id_type=MESH
        )

    eye = jnp.where(
        lax.broadcasted_iota(jnp.int32, (n, n), 0) == lax.broadcasted_iota(jnp.int32, (n, n), 1), 1.0, 0.0
    ).astype(F32)
    own = small.at[core, me_z]
    own[0:n, :] = dot(eye, c_in[...].reshape(tokens, n), ((1,), (1,)))
    own[n : 2 * n, :] = dot(eye, b_in[...].reshape(tokens, n), ((1,), (1,)))
    own[2 * n : 2 * n + groups, :] = jnp.exp(jnp.concatenate([wl[r] for r in range(rows)], axis=1))
    own[2 * n + groups :, :] = jnp.exp(jnp.concatenate([hl[r] for r in range(rows)], axis=1))

    def pack(source, target):
        for z in range(ha):
            for r in range(rows):
                v = source[r, :, z * lanes : (z + 1) * lanes].astype(F32)
                a, b = cross(v[: cols // 2], v[cols // 2 :])
                target[z * pair, r] = a
                target[z * pair + 1, r] = b

    pack(cot_in, msg_c)

    pl.semaphore_wait(barrier, owners + chips - 2)
    sends = []
    made_small = []
    for d in range(1, ha):
        z = lax.rem(me_z + d, ha)
        made_small.append(remote(own, own, s_small.at[d], r_small.at[d], {"ha": z}))
    for c in made_small:
        c.start()

    def spread(k, message, landing):
        made = []
        for d in range(1, owners):
            q = lax.rem(me_q + d, owners)
            made.append(remote(message.at[q], landing.at[me_q], s_in.at[k, d], r_in.at[k, d], column(q)))
        for c in made:
            c.start()
        landing[me_q] = message[me_q]
        sends.extend(made)
        return made

    def arrive(made):
        for c in made:
            c.wait_recv()

    got_c = spread(0, msg_c, land_c)
    pack(tok_in, msg_x)
    got_x = spread(1, msg_x, land_x)

    def place_tile(j, unused):
        l = lax.broadcasted_iota(jnp.int32, (lanes, pair * tokens), 0)
        o = lax.broadcasted_iota(jnp.int32, (lanes, pair * tokens), 1)
        hit = (lax.rem(o, cols) == j) & (lax.div(o, tokens) == lax.div(l, share))
        place[pl.ds(pl.multiple_of(j * lanes, lanes), lanes), :] = jnp.where(hit, 1.0, 0.0).astype(BF16)
        return unused

    lax.fori_loop(0, cols, place_tile, 0)
    hold[...] = jnp.zeros_like(hold)
    total[...] = jnp.zeros_like(total)

    arrive(made_small)
    made_core = []
    for e in range(1, pair):
        c = lax.rem(core + e, pair)
        made_core.append(
            remote(small.at[core], small.at[core], s_core.at[e], r_core.at[e], {"wa": chip * pair + c})
        )
    for c in made_core:
        c.start()
    arrive(made_core)
    sends.extend(made_small)
    sends.extend(made_core)

    at = lax.broadcasted_iota(jnp.int32, (pair * groups, lanes), 0)
    lane = lax.broadcasted_iota(jnp.int32, (pair * groups, lanes), 1)
    pick = jnp.where(at == lax.div(lane, share) * groups + mine, 1.0, 0.0).astype(F32)
    for target, first in ((wr, 2 * n), (hr, 2 * n + groups)):
        for z in range(ha):
            rates = jnp.concatenate([small[c, z, first : first + groups, :] for c in range(pair)], axis=0)
            target[z * rows : (z + 1) * rows] = dot(rates, pick, ((0,), (0,))).reshape(rows, cols, lanes)

    def row_products(i, unused):
        one = wr[i, 0:1, :]
        for j in range(1, cols):
            one = one * wr[i, j : j + 1, :]
        pw[i] = one
        return unused

    lax.fori_loop(0, high, row_products, 0)

    def chip_products(p, unused):
        a, b = pw[2 * p], pw[2 * p + 1]
        pc_msg[p] = jnp.where(low(a.shape), a * swap(a), b * swap(b))
        return unused

    lax.fori_loop(0, high // 2, chip_products, 0)
    made_pc = []
    for d in range(1, chips):
        c = lax.rem(chip + d, chips)
        made_pc.append(remote(pc_msg, pc_land.at[chip], s_pc.at[d], r_pc.at[d], across(c)))
    for c in made_pc:
        c.start()
    sends.extend(made_pc)

    keep = low((n, lanes))

    def widen(first, target):
        def one(z, unused):
            left = small[0, z, first : first + n, :]
            right = small[1, z, first : first + n, :]
            for r in range(rows):
                for j in range(cols):
                    t = r * cols + j
                    target[z * rows + r, j] = jnp.where(
                        keep,
                        jnp.broadcast_to(left[:, t : t + 1], (n, lanes)),
                        jnp.broadcast_to(right[:, t : t + 1], (n, lanes)),
                    )
            return unused

        lax.fori_loop(0, ha, one, 0)

    widen(0, cb)

    def unpack(landing, target):
        def one(i, unused):
            z, r = lax.div(i, rows), lax.rem(i, rows)
            a, b = cross(landing[z * pair, r], landing[z * pair + 1, r])
            target[i, 0 : cols // 2, :] = a
            target[i, cols // 2 :, :] = b
            return unused

        lax.fori_loop(0, high, one, 0)

    def wide_copy(k, z, message, landing, source, to):
        return remote(
            message.at[z], landing.at[source, z], s_wide.at[k, z, to], r_wide.at[k, z, source], across(to)
        )

    def wide_send(k, z, message, landing, backward):
        for c in range(chips):

            @pl.when(c < chip if backward else c > chip)
            def _():
                wide_copy(k, z, message, landing, chip, c).start()

    def wide_done(k, z, message, landing, backward):
        for c in range(chips):

            @pl.when(c < chip if backward else c > chip)
            def _():
                wide_copy(k, z, message, landing, chip, c).wait_send()

    def wide_arrive(k, z, message, landing, backward):
        for c in range(chips):

            @pl.when(c > chip if backward else c < chip)
            def _():
                wide_copy(k, z, message, landing, c, c).wait_recv()

    def join(z, ends, message, backward):
        for p in range(rows // 2):
            i = z * rows + 2 * p
            a = ends[i] + pw[i] * swap(ends[i])
            b = ends[i + 1] + pw[i + 1] * swap(ends[i + 1])
            message[z, p] = jnp.where(keep, a, swap(b)) if backward else jnp.where(keep, swap(a), b)

    def enter(z, ends, landing, target, backward):
        def step(t, carry):
            c = chips - 1 - t if backward else t
            return tuple(
                pc_land[c, z * (rows // 2) + p] * carry[p] + landing[c, z, p] for p in range(rows // 2)
            )

        zero = jnp.zeros((n, lanes), F32)
        carry = lax.fori_loop(0, chips - 1 - chip if backward else chip, step, (zero,) * (rows // 2))
        for p in range(rows // 2):
            for s in range(2):
                i = z * rows + 2 * p + s
                k = swap(carry[p]) if (s == 0) == backward else carry[p]
                after = swap(ends[i] + pw[i] * k)
                target[i] = jnp.where(keep, after, k) if backward else jnp.where(keep, k, after)

    arrive(got_c)
    unpack(land_c, cot)

    def col_scan(c, unused):
        z = ha - 1 - c

        def one(t, unused):
            i = z * rows + rows - 1 - t
            carry = jnp.zeros((n, lanes), F32)
            for j in range(cols - 1, -1, -1):
                grad = cb[i, j] * cot[i, j : j + 1, :] + hold[j]
                grads[i, j] = grad
                hold[j] = hr[i, j : j + 1, :] * grad
                carry = wr[i, j : j + 1, :] * (grad + carry)
            ends_b[i] = carry
            return unused

        lax.fori_loop(0, rows, one, 0)
        join(z, ends_b, wb_msg, True)
        wide_send(0, z, wb_msg, wb_land, True)
        return unused

    lax.fori_loop(0, ha, col_scan, 0)
    widen(n, bb)
    arrive(made_pc)

    arrive(got_x)
    unpack(land_x, x)

    def row_scan(z, unused):
        def one(r, unused):
            i = z * rows + r
            carry = bb[i, 0] * x[i, 0:1, :]
            for j in range(1, cols):
                carry = wr[i, j : j + 1, :] * carry + bb[i, j] * x[i, j : j + 1, :]
            ends_f[i] = carry
            return unused

        lax.fori_loop(0, rows, one, 0)
        join(z, ends_f, wf_msg, False)
        wide_send(1, z, wf_msg, wf_land, False)
        return unused

    lax.fori_loop(0, ha, row_scan, 0)

    def halves(v):
        top = v.astype(BF16)
        return top, (v - top.astype(F32)).astype(BF16)

    def at_row(shape, r):
        return lax.div(lax.broadcasted_iota(jnp.int32, shape, 1), cols) == r

    def home(k, z, e, message, landing):
        q = z * pair + e
        return remote(message.at[q], landing.at[me_q], s_out.at[k, q], r_out.at[k, me_q], column(q))

    def go_home(k, z, message, landing):
        for e in range(pair):

            @pl.when(z * pair + e != me_q)
            def _():
                home(k, z, e, message, landing).start()

            @pl.when(z * pair + e == me_q)
            def _():
                landing[me_q] = message[z * pair + e]

    def rows_done(c, unused):
        z = ha - 1 - c
        wide_arrive(0, z, wb_msg, wb_land, True)
        enter(z, ends_b, wb_land, cin_b, True)

        def one(r, unused):
            i = z * rows + r
            carry = cin_b[i]
            for j in range(cols - 1, -1, -1):
                grad = grads[i, j] + carry
                rows_grad[i, j] = grad
                carry = wr[i, j : j + 1, :] * grad
                tok_rows[r, j : j + 1, :] = jnp.sum(grad * bb[i, j], axis=0, keepdims=True)
                top, rest = halves(grad * x[i, j : j + 1, :])
                prod_b[r, 0:n, j * lanes : (j + 1) * lanes] = top
                prod_b[r, n : 2 * n, j * lanes : (j + 1) * lanes] = rest
            return unused

        lax.fori_loop(0, rows, one, 0)
        for r in range(rows):
            a, b = cross(tok_rows[r, 0 : cols // 2, :], tok_rows[r, cols // 2 :, :])
            tok_msg[z * pair, r] = a
            tok_msg[z * pair + 1, r] = b
        go_home(0, z, tok_msg, tok_home)
        sums = jnp.dot(
            prod_b[...].reshape(rows * 2 * n, cols * lanes), place[...], preferred_element_type=F32
        ).reshape(rows, 2 * n, pair * tokens)
        for e in range(pair):
            out = jnp.zeros((n, tokens), F32)
            for r in range(rows):
                v = sums[r, :, e * tokens : (e + 1) * tokens]
                out = jnp.where(at_row(out.shape, r), v[:n] + v[n:], out)
            in_msg[z * pair + e] = out
        go_home(1, z, in_msg, in_home)
        return unused

    lax.fori_loop(0, ha, rows_done, 0)

    sub = lax.broadcasted_iota(jnp.int32, (8, tokens), 0)

    def cols_done(z, unused):
        wide_arrive(1, z, wf_msg, wf_land, False)
        enter(z, ends_f, wf_land, cin_f, False)

        def one(r, unused):
            i = z * rows + r
            carry = cin_f[i]
            for j in range(cols):
                w = rows_grad[i, j] * carry
                carry = wr[i, j : j + 1, :] * carry + bb[i, j] * x[i, j : j + 1, :]
                before = total[j]
                h = grads[i, j] * before
                now = hr[i, j : j + 1, :] * before + carry
                total[j] = now
                where = slice(j * lanes, (j + 1) * lanes)
                top, rest = halves(now * cot[i, j : j + 1, :])
                prod_f[r, 0:n, where] = top
                prod_f[r, n : 2 * n, where] = rest
                both = jnp.concatenate([w[: n // 2] + w[n // 2 :], h[: n // 2] + h[n // 2 :]], axis=0)
                top, rest = halves(both)
                prod_f[r, 2 * n : 3 * n, where] = top
                prod_f[r, 3 * n : 4 * n, where] = rest
            return unused

        lax.fori_loop(0, rows, one, 0)
        sums = jnp.dot(
            prod_f[...].reshape(rows * 4 * n, cols * lanes), place[...], preferred_element_type=F32
        ).reshape(rows, 4 * n, pair * tokens)
        for e in range(pair):
            out = jnp.zeros((n, tokens), F32)
            both = jnp.zeros((n, tokens), F32)
            for r in range(rows):
                v = sums[r, :, e * tokens : (e + 1) * tokens]
                out = jnp.where(at_row(out.shape, r), v[:n] + v[n : 2 * n], out)
                both = jnp.where(at_row(out.shape, r), v[2 * n : 3 * n] + v[3 * n :], both)
            w = jnp.sum(both[: n // 2], axis=0, keepdims=True)
            h = jnp.sum(both[n // 2 :], axis=0, keepdims=True)
            fin_msg[z * pair + e, 0:n] = out
            fin_msg[z * pair + e, n:] = jnp.where(sub == 0, w, jnp.where(sub == 1, h, 0.0))
        go_home(2, z, fin_msg, fin_home)
        return unused

    lax.fori_loop(0, ha, cols_done, 0)

    for c in sends:
        c.wait_send()

    def finish(z, unused):
        wide_done(0, z, wb_msg, wb_land, True)
        wide_done(1, z, wf_msg, wf_land, False)
        for k, message, landing in ((0, tok_msg, tok_home), (1, in_msg, in_home), (2, fin_msg, fin_home)):
            for e in range(pair):

                @pl.when(z * pair + e != me_q)
                def _():
                    home(k, z, e, message, landing).wait_send()

                @pl.when(z * pair + e != me_q)
                def _():
                    q = z * pair + e
                    remote(message.at[q], landing.at[q], s_out.at[k, q], r_out.at[k, q], column(q)).wait_recv()

        return unused

    lax.fori_loop(0, ha, finish, 0)


def at_home(ha, pair, tok_home, in_home, fin_home, wl, hl, tok_out, in_out, so_out, wg_out, hg_out):
    rows, cols, channels = tok_out.shape
    n = in_out.shape[1]
    groups = wl.shape[1]
    lanes = channels // ha
    owners = ha * pair
    tokens = rows * cols
    for z in range(ha):
        for r in range(rows):
            a, b = cross(tok_home[z * pair, r], tok_home[z * pair + 1, r])
            tok_out[r, 0 : cols // 2, z * lanes : (z + 1) * lanes] = a
            tok_out[r, cols // 2 :, z * lanes : (z + 1) * lanes] = b
    in_sum, so_sum = in_home[0], fin_home[0, 0:n]
    for q in range(1, owners):
        in_sum = in_sum + in_home[q]
        so_sum = so_sum + fin_home[q, 0:n]
    in_out[...] = in_sum.T
    so_out[...] = so_sum.T
    sub = lax.broadcasted_iota(jnp.int32, (groups, tokens), 0)
    for k, decay, out in ((0, wl, wg_out), (1, hl, hg_out)):
        rate_sum = jnp.zeros((groups, tokens), F32)
        for q in range(owners):
            g = q * groups // owners
            rate_sum = rate_sum + jnp.where(sub == g, fin_home[q, n + k : n + k + 1, :], 0.0)
        for r in range(rows):
            out[r] = rate_sum[:, r * cols : (r + 1) * cols] * jnp.exp(decay[r])


def per_device(ha, wa, tokens, cotangent, state_in, state_out, width_decay, height_decay):
    rows, cols, channels = tokens.shape
    n = state_in.shape[2]
    groups = width_decay.shape[2]
    pair = 2
    chips = wa // pair
    owners = ha * pair
    lanes = channels // ha
    high = ha * rows
    count = rows * cols
    vmem = pl.BlockSpec(memory_space=pltpu.VMEM)
    room = lambda *shape: pltpu.VMEM(shape, F32)
    sems = lambda *shape: pltpu.SemaphoreType.DMA(shape)
    wl = jnp.swapaxes(width_decay, 1, 2)
    hl = jnp.swapaxes(height_decay, 1, 2)
    message = (owners, rows, cols // 2, lanes)
    state = (high, cols, n, lanes)
    ends = (high, n, lanes)
    wide = (ha, rows // 2, n, lanes)
    homes = pl.pallas_call(
        functools.partial(exchange, ha, chips, pair),
        out_shape=[
            jax.ShapeDtypeStruct(message, F32),
            jax.ShapeDtypeStruct((owners, n, count), F32),
            jax.ShapeDtypeStruct((owners, n + 8, count), F32),
        ],
        in_specs=[vmem] * 6,
        out_specs=[vmem] * 3,
        scratch_shapes=[room(*message) for _ in range(4)]
        + [room(pair, ha, 2 * n + 2 * groups, count)]
        + [room(high, cols, lanes) for _ in range(4)]
        + [room(*state) for _ in range(4)]
        + [room(cols, n, lanes) for _ in range(2)]
        + [room(*ends) for _ in range(4)]
        + [room(high, 1, lanes), room(high // 2, 1, lanes), room(chips, high // 2, 1, lanes)]
        + [room(*wide), room(chips, *wide), room(*wide), room(chips, *wide)]
        + [
            pltpu.VMEM((cols * lanes, pair * count), BF16),
            pltpu.VMEM((rows, 2 * n, cols * lanes), BF16),
            pltpu.VMEM((rows, 4 * n, cols * lanes), BF16),
            room(rows, cols, lanes),
            room(*message),
            room(owners, n, count),
            room(owners, n + 8, count),
        ]
        + [sems(ha), sems(ha), sems(pair), sems(pair)]
        + [sems(2, owners), sems(2, owners), sems(chips), sems(chips)]
        + [sems(2, ha, chips), sems(2, ha, chips), sems(3, owners), sems(3, owners)],
        compiler_params=pltpu.CompilerParams(
            collective_id=0, has_side_effects=True, vmem_limit_bytes=56 * 1024 * 1024
        ),
        name="exchange",
    )(tokens, cotangent, state_in, state_out, wl, hl)
    result = pl.pallas_call(
        functools.partial(at_home, ha, pair),
        out_shape=[
            jax.ShapeDtypeStruct((rows, cols, channels), F32),
            jax.ShapeDtypeStruct((count, n), F32),
            jax.ShapeDtypeStruct((count, n), F32),
            jax.ShapeDtypeStruct((rows, groups, cols), F32),
            jax.ShapeDtypeStruct((rows, groups, cols), F32),
        ],
        in_specs=[vmem] * 5,
        out_specs=[vmem] * 5,
        name="at_home",
    )(*homes, wl, hl)
    return (
        result[0],
        result[1].reshape(rows, cols, n),
        result[2].reshape(rows, cols, n),
        jnp.swapaxes(result[3], 1, 2),
        jnp.swapaxes(result[4], 1, 2),
    )


def solution(mesh):
    spec = P("ha", "wa", None)
    return jax.shard_map(
        functools.partial(per_device, mesh.shape["ha"], mesh.shape["wa"]),
        mesh=mesh,
        in_specs=(spec,) * 6,
        out_specs=(spec,) * 5,
        check_vma=False,
    )
```

```python
import functools

import jax
import jax.numpy as jnp
from jax import lax
from jax.experimental import pallas as pl
from jax.experimental.pallas import tpu as pltpu
from jax.sharding import PartitionSpec as P

MESH = pl.DeviceIdType.MESH
F32 = jnp.float32
BF16 = jnp.bfloat16
HIGHEST = lax.Precision.HIGHEST


def swap(v):
    half = v.shape[-1] // 2
    if v.shape[-1] % 128 == 0:
        return pltpu.roll(v, half, v.ndim - 1)
    return jnp.concatenate([v[..., half:], v[..., :half]], axis=-1)


def low(shape):
    return lax.broadcasted_iota(jnp.int32, shape, len(shape) - 1) < shape[-1] // 2


def cross(a, b):
    keep = low(a.shape)
    return jnp.where(keep, a, swap(b)), jnp.where(keep, swap(a), b)


def exchange(
    ha,
    chips,
    pair,
    tok_in,
    cot_in,
    b_in,
    c_in,
    wl,
    hl,
    tok_home,
    in_home,
    fin_home,
    msg_c,
    msg_x,
    land_c,
    land_x,
    small,
    cot,
    x,
    wr,
    hr,
    cb,
    bb,
    grads,
    rows_grad,
    hold,
    total,
    ends_b,
    ends_f,
    cin_b,
    cin_f,
    pw,
    pc_msg,
    pc_land,
    wb_msg,
    wb_land,
    wf_msg,
    wf_land,
    place,
    prod,
    part_w,
    part_h,
    tok_rows,
    tok_msg,
    in_msg,
    fin_msg,
    s_small,
    r_small,
    s_core,
    r_core,
    s_in,
    r_in,
    s_pc,
    r_pc,
    s_wide,
    r_wide,
    s_out,
    r_out,
):
    rows, cols, channels = tok_in.shape
    n = b_in.shape[2]
    groups = wl.shape[1]
    lanes = channels // ha
    share = lanes // pair
    owners = ha * pair
    high = ha * rows
    tokens = rows * cols
    me_z = lax.axis_index("ha")
    me_w = lax.axis_index("wa")
    chip = me_w // pair
    core = lax.rem(me_w, pair)
    me_q = me_z * pair + core
    mine = lax.div(me_q * share, channels // groups)

    def column(q):
        return {"ha": lax.div(q, pair), "wa": chip * pair + lax.rem(q, pair)}

    def across(c):
        return {"wa": c * pair + core}

    def remote(src, dst, ss, rs, device):
        return pltpu.make_async_remote_copy(
            src_ref=src, dst_ref=dst, send_sem=ss, recv_sem=rs, device_id=device, device_id_type=MESH
        )

    def dot(a, b, dims):
        return lax.dot_general(a, b, (dims, ((), ())), precision=HIGHEST, preferred_element_type=F32)

    barrier = pltpu.get_barrier_semaphore()
    for d in range(1, owners):
        pl.semaphore_signal(
            barrier, inc=1, device_id=column(lax.rem(me_q + d, owners)), device_id_type=MESH
        )
    for d in range(1, chips):
        pl.semaphore_signal(
            barrier, inc=1, device_id=across(lax.rem(chip + d, chips)), device_id_type=MESH
        )

    eye = jnp.where(
        lax.broadcasted_iota(jnp.int32, (n, n), 0) == lax.broadcasted_iota(jnp.int32, (n, n), 1), 1.0, 0.0
    ).astype(F32)
    own = small.at[core, me_z]
    own[0:n, :] = dot(eye, c_in[...].reshape(tokens, n), ((1,), (1,)))
    own[n : 2 * n, :] = dot(eye, b_in[...].reshape(tokens, n), ((1,), (1,)))
    own[2 * n : 2 * n + groups, :] = jnp.exp(jnp.concatenate([wl[r] for r in range(rows)], axis=1))
    own[2 * n + groups :, :] = jnp.exp(jnp.concatenate([hl[r] for r in range(rows)], axis=1))

    def pack(source, target):
        for z in range(ha):
            for r in range(rows):
                v = source[r, :, z * lanes : (z + 1) * lanes].astype(F32)
                a, b = cross(v[: cols // 2], v[cols // 2 :])
                target[z * pair, r] = a
                target[z * pair + 1, r] = b

    pack(cot_in, msg_c)

    pl.semaphore_wait(barrier, owners + chips - 2)
    sends = []
    made_small = []
    for d in range(1, ha):
        z = lax.rem(me_z + d, ha)
        made_small.append(remote(own, own, s_small.at[d], r_small.at[d], {"ha": z}))
    for c in made_small:
        c.start()

    def spread(k, message, landing):
        made = []
        for d in range(1, owners):
            q = lax.rem(me_q + d, owners)
            made.append(remote(message.at[q], landing.at[me_q], s_in.at[k, q], r_in.at[k, me_q], column(q)))
        for c in made:
            c.start()
        landing[me_q] = message[me_q]
        sends.extend(made)

    def gather_in(k, z, message, landing, target):
        for e in range(pair):
            q = z * pair + e

            @pl.when(q != me_q)
            def _():
                remote(message.at[q], landing.at[q], s_in.at[k, q], r_in.at[k, q], column(q)).wait_recv()

        for r in range(rows):
            a, b = cross(landing[z * pair, r], landing[z * pair + 1, r])
            target[z * rows + r, 0 : cols // 2, :] = a
            target[z * rows + r, cols // 2 :, :] = b

    def arrive(made):
        for c in made:
            c.wait_recv()

    spread(0, msg_c, land_c)
    pack(tok_in, msg_x)
    spread(1, msg_x, land_x)

    l = lax.broadcasted_iota(jnp.int32, (lanes, pair * tokens), 0)
    o = lax.broadcasted_iota(jnp.int32, (lanes, pair * tokens), 1)
    column_of = jnp.where(lax.div(o, tokens) == lax.div(l, share), lax.rem(o, cols), -1)

    def place_tile(j, unused):
        ones = jnp.where(column_of == j, 1.0, 0.0).astype(BF16)
        place[pl.ds(pl.multiple_of(j * lanes, lanes), lanes), :] = ones
        return unused

    lax.fori_loop(0, cols, place_tile, 0)
    hold[...] = jnp.zeros_like(hold)
    total[...] = jnp.zeros_like(total)

    arrive(made_small)
    made_core = []
    for e in range(1, pair):
        c = lax.rem(core + e, pair)
        made_core.append(
            remote(small.at[core], small.at[core], s_core.at[e], r_core.at[e], {"wa": chip * pair + c})
        )
    for c in made_core:
        c.start()
    arrive(made_core)
    sends.extend(made_small)
    sends.extend(made_core)

    at = lax.broadcasted_iota(jnp.int32, (pair * groups, lanes), 0)
    lane = lax.broadcasted_iota(jnp.int32, (pair * groups, lanes), 1)
    pick = jnp.where(at == lax.div(lane, share) * groups + mine, 1.0, 0.0).astype(F32)
    for target, first in ((wr, 2 * n), (hr, 2 * n + groups)):
        for z in range(ha):
            rates = jnp.concatenate([small[c, z, first : first + groups, :] for c in range(pair)], axis=0)
            target[z * rows : (z + 1) * rows] = dot(rates, pick, ((0,), (0,))).reshape(rows, cols, lanes)

    def products(z, unused):
        rates = []
        for r in range(rows):
            i = z * rows + r
            one = wr[i]
            size = cols
            while size > 8:
                size //= 2
                one = one[:size] * one[size:]
            while size > 1:
                size //= 2
                one = one * pltpu.roll(one, size, 0)
            pw[i] = one[0:1]
            rates.append(one[0:1] * swap(one)[0:1])
        for p in range(rows // 2):
            pc_msg[z * (rows // 2) + p] = jnp.where(low((1, lanes)), rates[2 * p], rates[2 * p + 1])
        return unused

    lax.fori_loop(0, ha, products, 0)
    made_pc = []
    for d in range(1, chips):
        c = lax.rem(chip + d, chips)
        made_pc.append(remote(pc_msg, pc_land.at[chip], s_pc.at[d], r_pc.at[d], across(c)))
    for c in made_pc:
        c.start()
    sends.extend(made_pc)

    keep = low((n, lanes))

    def widen(first, target):
        def one(z, unused):
            left = small[0, z, first : first + n, :]
            right = small[1, z, first : first + n, :]
            for t in range(tokens):
                target[z * rows + t // cols, t % cols] = jnp.where(
                    keep,
                    jnp.broadcast_to(left[:, t : t + 1], (n, lanes)),
                    jnp.broadcast_to(right[:, t : t + 1], (n, lanes)),
                )
            return unused

        return one

    lax.fori_loop(0, ha, widen(0, cb), 0)
    lax.fori_loop(0, ha // 4, widen(n, bb), 0)

    def wide_copy(k, z, message, landing, source, to):
        return remote(
            message.at[z], landing.at[source, z], s_wide.at[k, z, to], r_wide.at[k, z, source], across(to)
        )

    def wide_send(k, z, message, landing, backward):
        for c in range(chips):

            @pl.when(c < chip if backward else c > chip)
            def _():
                wide_copy(k, z, message, landing, chip, c).start()

    def wide_done(k, z, message, landing, backward):
        for c in range(chips):

            @pl.when(c < chip if backward else c > chip)
            def _():
                wide_copy(k, z, message, landing, chip, c).wait_send()

    def wide_arrive(k, z, message, landing, backward):
        for c in range(chips):

            @pl.when(c > chip if backward else c < chip)
            def _():
                wide_copy(k, z, message, landing, c, c).wait_recv()

    def join(z, ends, message, backward):
        for p in range(rows // 2):
            i = z * rows + 2 * p
            a = ends[i] + pw[i] * swap(ends[i])
            b = ends[i + 1] + pw[i + 1] * swap(ends[i + 1])
            message[z, p] = jnp.where(keep, a, swap(b)) if backward else jnp.where(keep, swap(a), b)

    def enter(z, ends, landing, target, backward):
        def step(t, carry):
            c = chips - 1 - t if backward else t
            return tuple(
                pc_land[c, z * (rows // 2) + p] * carry[p] + landing[c, z, p] for p in range(rows // 2)
            )

        zero = jnp.zeros((n, lanes), F32)
        carry = lax.fori_loop(0, chips - 1 - chip if backward else chip, step, (zero,) * (rows // 2))
        for p in range(rows // 2):
            for s in range(2):
                i = z * rows + 2 * p + s
                k = swap(carry[p]) if (s == 0) == backward else carry[p]
                after = swap(ends[i] + pw[i] * k)
                target[i] = jnp.where(keep, after, k) if backward else jnp.where(keep, k, after)

    def col_scan(c, unused):
        z = ha - 1 - c
        gather_in(0, z, msg_c, land_c, cot)

        def one(t, unused):
            i = z * rows + rows - 1 - t
            carry = jnp.zeros((n, lanes), F32)
            for j in range(cols - 1, -1, -1):
                grad = cb[i, j] * cot[i, j : j + 1, :] + hold[j]
                grads[i, j] = grad
                hold[j] = hr[i, j : j + 1, :] * grad
                carry = wr[i, j : j + 1, :] * (grad + carry)
            ends_b[i] = carry
            return unused

        lax.fori_loop(0, rows, one, 0, unroll=True)
        join(z, ends_b, wb_msg, True)
        wide_send(0, z, wb_msg, wb_land, True)
        return unused

    lax.fori_loop(0, ha, col_scan, 0)
    lax.fori_loop(ha // 4, ha, widen(n, bb), 0)
    arrive(made_pc)

    def row_scan(c, unused):
        z = lax.rem(me_z + c, ha)
        gather_in(1, z, msg_x, land_x, x)

        def one(r, unused):
            i = z * rows + r
            carry = bb[i, 0] * x[i, 0:1, :]
            for j in range(1, cols):
                carry = wr[i, j : j + 1, :] * carry + bb[i, j] * x[i, j : j + 1, :]
            ends_f[i] = carry
            return unused

        lax.fori_loop(0, rows, one, 0, unroll=True)
        join(z, ends_f, wf_msg, False)
        wide_send(1, z, wf_msg, wf_land, False)
        return unused

    lax.fori_loop(0, ha, row_scan, 0)

    def keep_product(r, j, v):
        top = v.astype(BF16)
        prod[r, 0:n, j * lanes : (j + 1) * lanes] = top
        prod[r, n:, j * lanes : (j + 1) * lanes] = (v - top.astype(F32)).astype(BF16)

    row_of = lax.div(lax.broadcasted_iota(jnp.int32, (n, tokens), 1), cols)

    def channel_sums(message, z):
        v = jnp.dot(prod[...].reshape(rows * 2 * n, cols * lanes), place[...], preferred_element_type=F32)
        for e in range(pair):
            out = jnp.zeros((n, tokens), F32)
            for r in range(rows):
                part = v[r * 2 * n : (r + 1) * 2 * n, e * tokens : (e + 1) * tokens]
                out = jnp.where(row_of == r, part[:n] + part[n:], out)
            message[z * pair + e, 0:n] = out

    def group_sums():
        both = jnp.concatenate([part_w[...], part_h[...]], axis=0)
        top = both.astype(BF16)
        rest = (both - top.astype(F32)).astype(BF16)
        v = jnp.dot(jnp.concatenate([top, rest], axis=0), place[...], preferred_element_type=F32)
        v = v[: 2 * rows] + v[2 * rows :]
        sub = lax.broadcasted_iota(jnp.int32, (rows, tokens), 0)
        row = lax.div(lax.broadcasted_iota(jnp.int32, (rows, tokens), 1), cols)
        out = []
        for e in range(pair):
            part = v[:, e * tokens : (e + 1) * tokens]
            out.append(
                [
                    jnp.sum(jnp.where(sub == row, part[k * rows : (k + 1) * rows], 0.0), axis=0, keepdims=True)
                    for k in range(2)
                ]
            )
        return out

    def home(k, z, e, message, landing):
        q = z * pair + e
        return remote(message.at[q], landing.at[me_q], s_out.at[k, q], r_out.at[k, me_q], column(q))

    def go_home(k, z, message, landing):
        for e in range(pair):

            @pl.when(z * pair + e != me_q)
            def _():
                home(k, z, e, message, landing).start()

            @pl.when(z * pair + e == me_q)
            def _():
                landing[me_q] = message[z * pair + e]

    def rows_done(c, unused):
        z = ha - 1 - c
        wide_arrive(0, z, wb_msg, wb_land, True)
        enter(z, ends_b, wb_land, cin_b, True)

        def one(r, unused):
            i = z * rows + r
            carry = cin_b[i]
            for j in range(cols - 1, -1, -1):
                grad = grads[i, j] + carry
                rows_grad[i, j] = grad
                carry = wr[i, j : j + 1, :] * grad
                tok_rows[r, j : j + 1, :] = jnp.sum(grad * bb[i, j], axis=0, keepdims=True)
                keep_product(r, j, grad * x[i, j : j + 1, :])
            return unused

        lax.fori_loop(0, rows, one, 0, unroll=True)
        for r in range(rows):
            a, b = cross(tok_rows[r, 0 : cols // 2, :], tok_rows[r, cols // 2 :, :])
            tok_msg[z * pair, r] = a
            tok_msg[z * pair + 1, r] = b
        go_home(0, z, tok_msg, tok_home)
        channel_sums(in_msg, z)
        go_home(1, z, in_msg, in_home)
        return unused

    lax.fori_loop(0, ha, rows_done, 0)

    sub = lax.broadcasted_iota(jnp.int32, (8, tokens), 0)

    def cols_done(z, unused):
        wide_arrive(1, z, wf_msg, wf_land, False)
        enter(z, ends_f, wf_land, cin_f, False)

        def one(r, unused):
            i = z * rows + r
            carry = cin_f[i]
            for j in range(cols):
                w = rows_grad[i, j] * carry
                carry = wr[i, j : j + 1, :] * carry + bb[i, j] * x[i, j : j + 1, :]
                before = total[j]
                h = grads[i, j] * before
                now = hr[i, j : j + 1, :] * before + carry
                total[j] = now
                keep_product(r, j, now * cot[i, j : j + 1, :])
                part_w[pl.ds(r, 1), j * lanes : (j + 1) * lanes] = jnp.sum(w, axis=0, keepdims=True)
                part_h[pl.ds(r, 1), j * lanes : (j + 1) * lanes] = jnp.sum(h, axis=0, keepdims=True)
            return unused

        lax.fori_loop(0, rows, one, 0, unroll=True)
        channel_sums(fin_msg, z)
        for e, (w, h) in enumerate(group_sums()):
            fin_msg[z * pair + e, n:] = jnp.where(sub == 0, w, jnp.where(sub == 1, h, 0.0))
        go_home(2, z, fin_msg, fin_home)
        return unused

    lax.fori_loop(0, ha, cols_done, 0)

    for c in sends:
        c.wait_send()

    def finish(z, unused):
        wide_done(0, z, wb_msg, wb_land, True)
        wide_done(1, z, wf_msg, wf_land, False)
        for k, message, landing in ((0, tok_msg, tok_home), (1, in_msg, in_home), (2, fin_msg, fin_home)):
            for e in range(pair):

                @pl.when(z * pair + e != me_q)
                def _():
                    home(k, z, e, message, landing).wait_send()

                @pl.when(z * pair + e != me_q)
                def _():
                    q = z * pair + e
                    remote(message.at[q], landing.at[q], s_out.at[k, q], r_out.at[k, q], column(q)).wait_recv()

        return unused

    lax.fori_loop(0, ha, finish, 0)


def at_home(ha, pair, tok_home, in_home, fin_home, wl, hl, tok_out, in_out, so_out, wg_out, hg_out):
    rows, cols, channels = tok_out.shape
    n = in_out.shape[1]
    groups = wl.shape[1]
    lanes = channels // ha
    owners = ha * pair
    tokens = rows * cols
    for z in range(ha):
        for r in range(rows):
            a, b = cross(tok_home[z * pair, r], tok_home[z * pair + 1, r])
            tok_out[r, 0 : cols // 2, z * lanes : (z + 1) * lanes] = a
            tok_out[r, cols // 2 :, z * lanes : (z + 1) * lanes] = b
    in_sum, so_sum = in_home[0], fin_home[0, 0:n]
    for q in range(1, owners):
        in_sum = in_sum + in_home[q]
        so_sum = so_sum + fin_home[q, 0:n]
    in_out[...] = in_sum.T
    so_out[...] = so_sum.T
    sub = lax.broadcasted_iota(jnp.int32, (groups, tokens), 0)
    for k, decay, out in ((0, wl, wg_out), (1, hl, hg_out)):
        rate_sum = jnp.zeros((groups, tokens), F32)
        for q in range(owners):
            g = q * groups // owners
            rate_sum = rate_sum + jnp.where(sub == g, fin_home[q, n + k : n + k + 1, :], 0.0)
        for r in range(rows):
            out[r] = rate_sum[:, r * cols : (r + 1) * cols] * jnp.exp(decay[r])


def per_device(ha, wa, tokens, cotangent, state_in, state_out, width_decay, height_decay):
    rows, cols, channels = tokens.shape
    n = state_in.shape[2]
    groups = width_decay.shape[2]
    pair = 2
    chips = wa // pair
    owners = ha * pair
    lanes = channels // ha
    high = ha * rows
    count = rows * cols
    vmem = pl.BlockSpec(memory_space=pltpu.VMEM)
    room = lambda *shape: pltpu.VMEM(shape, F32)
    sems = lambda *shape: pltpu.SemaphoreType.DMA(shape)
    wl = jnp.swapaxes(width_decay, 1, 2)
    hl = jnp.swapaxes(height_decay, 1, 2)
    message = (owners, rows, cols // 2, lanes)
    state = (high, cols, n, lanes)
    ends = (high, n, lanes)
    wide = (ha, rows // 2, n, lanes)
    homes = pl.pallas_call(
        functools.partial(exchange, ha, chips, pair),
        out_shape=[
            jax.ShapeDtypeStruct(message, F32),
            jax.ShapeDtypeStruct((owners, n, count), F32),
            jax.ShapeDtypeStruct((owners, n + 8, count), F32),
        ],
        in_specs=[vmem] * 6,
        out_specs=[vmem] * 3,
        scratch_shapes=[room(*message) for _ in range(4)]
        + [room(pair, ha, 2 * n + 2 * groups, count)]
        + [room(high, cols, lanes) for _ in range(4)]
        + [room(*state) for _ in range(4)]
        + [room(cols, n, lanes) for _ in range(2)]
        + [room(*ends) for _ in range(4)]
        + [room(high, 1, lanes), room(high // 2, 1, lanes), room(chips, high // 2, 1, lanes)]
        + [room(*wide), room(chips, *wide), room(*wide), room(chips, *wide)]
        + [
            pltpu.VMEM((cols * lanes, pair * count), BF16),
            pltpu.VMEM((rows, 2 * n, cols * lanes), BF16),
            room(rows, cols * lanes),
            room(rows, cols * lanes),
            room(rows, cols, lanes),
            room(*message),
            room(owners, n, count),
            room(owners, n + 8, count),
        ]
        + [sems(ha), sems(ha), sems(pair), sems(pair)]
        + [sems(2, owners), sems(2, owners), sems(chips), sems(chips)]
        + [sems(2, ha, chips), sems(2, ha, chips), sems(3, owners), sems(3, owners)],
        compiler_params=pltpu.CompilerParams(
            collective_id=0, has_side_effects=True, vmem_limit_bytes=56 * 1024 * 1024
        ),
        name="exchange",
    )(tokens, cotangent, state_in, state_out, wl, hl)
    result = pl.pallas_call(
        functools.partial(at_home, ha, pair),
        out_shape=[
            jax.ShapeDtypeStruct((rows, cols, channels), F32),
            jax.ShapeDtypeStruct((count, n), F32),
            jax.ShapeDtypeStruct((count, n), F32),
            jax.ShapeDtypeStruct((rows, groups, cols), F32),
            jax.ShapeDtypeStruct((rows, groups, cols), F32),
        ],
        in_specs=[vmem] * 5,
        out_specs=[vmem] * 5,
        name="at_home",
    )(*homes, wl, hl)
    return (
        result[0],
        result[1].reshape(rows, cols, n),
        result[2].reshape(rows, cols, n),
        jnp.swapaxes(result[3], 1, 2),
        jnp.swapaxes(result[4], 1, 2),
    )


def solution(mesh):
    spec = P("ha", "wa", None)
    return jax.shard_map(
        functools.partial(per_device, mesh.shape["ha"], mesh.shape["wa"]),
        mesh=mesh,
        in_specs=(spec,) * 6,
        out_specs=(spec,) * 5,
        check_vma=False,
    )
```

```python
import functools

import jax
import jax.numpy as jnp
from jax import lax
from jax.experimental import pallas as pl
from jax.experimental.pallas import tpu as pltpu
from jax.sharding import PartitionSpec as P

MESH = pl.DeviceIdType.MESH
F32 = jnp.float32
BF16 = jnp.bfloat16
HIGHEST = lax.Precision.HIGHEST


def swap(v):
    half = v.shape[-1] // 2
    if v.shape[-1] % 128 == 0:
        return pltpu.roll(v, half, v.ndim - 1)
    return jnp.concatenate([v[..., half:], v[..., :half]], axis=-1)


def low(shape):
    return lax.broadcasted_iota(jnp.int32, shape, len(shape) - 1) < shape[-1] // 2


def cross(a, b):
    keep = low(a.shape)
    return jnp.where(keep, a, swap(b)), jnp.where(keep, swap(a), b)


def exchange(
    ha,
    chips,
    pair,
    tok_far,
    cot_far,
    b_far,
    c_far,
    wl_far,
    hl_far,
    tok_home,
    in_home,
    fin_home,
    tok_in,
    cot_in,
    b_in,
    c_in,
    wl,
    hl,
    msg_c,
    msg_x,
    land_c,
    land_x,
    small,
    cot,
    x,
    wr,
    hr,
    cb,
    bb,
    grads,
    rows_grad,
    hold,
    total,
    ends_b,
    ends_f,
    cin_b,
    cin_f,
    pw,
    pc_msg,
    pc_land,
    wb_msg,
    wb_land,
    wf_msg,
    wf_land,
    place,
    prod_in,
    prod,
    part_w,
    part_h,
    tok_rows,
    tok_msg,
    in_msg,
    fin_msg,
    s_small,
    r_small,
    s_core,
    r_core,
    s_in,
    r_in,
    s_pc,
    r_pc,
    s_wide,
    r_wide,
    s_out,
    r_out,
    s_load,
    s_own,
):
    rows, cols, channels = tok_in.shape
    n = b_in.shape[2]
    groups = wl.shape[1]
    lanes = channels // ha
    share = lanes // pair
    owners = ha * pair
    high = ha * rows
    tokens = rows * cols
    me_z = lax.axis_index("ha")
    me_w = lax.axis_index("wa")
    chip = me_w // pair
    core = lax.rem(me_w, pair)
    me_q = me_z * pair + core
    mine = lax.div(me_q * share, channels // groups)

    def column(q):
        return {"ha": lax.div(q, pair), "wa": chip * pair + lax.rem(q, pair)}

    def across(c):
        return {"wa": c * pair + core}

    def remote(src, dst, ss, rs, device):
        return pltpu.make_async_remote_copy(
            src_ref=src, dst_ref=dst, send_sem=ss, recv_sem=rs, device_id=device, device_id_type=MESH
        )

    def dot(a, b, dims):
        return lax.dot_general(a, b, (dims, ((), ())), precision=HIGHEST, preferred_element_type=F32)

    barrier = pltpu.get_barrier_semaphore()
    for d in range(1, owners):
        pl.semaphore_signal(
            barrier, inc=1, device_id=column(lax.rem(me_q + d, owners)), device_id_type=MESH
        )
    for d in range(1, chips):
        pl.semaphore_signal(
            barrier, inc=1, device_id=across(lax.rem(chip + d, chips)), device_id_type=MESH
        )

    loads = [
        pltpu.make_async_copy(far, near, s_load.at[k])
        for k, (far, near) in enumerate(
            ((c_far, c_in), (b_far, b_in), (wl_far, wl), (hl_far, hl), (cot_far, cot_in), (tok_far, tok_in))
        )
    ]
    for c in loads:
        c.start()
    for c in loads[:4]:
        c.wait()

    eye = jnp.where(
        lax.broadcasted_iota(jnp.int32, (n, n), 0) == lax.broadcasted_iota(jnp.int32, (n, n), 1), 1.0, 0.0
    ).astype(F32)
    own = small.at[core, me_z]
    own[0:n, :] = dot(eye, c_in[...].reshape(tokens, n), ((1,), (1,)))
    own[n : 2 * n, :] = dot(eye, b_in[...].reshape(tokens, n), ((1,), (1,)))
    own[2 * n : 2 * n + groups, :] = jnp.exp(jnp.concatenate([wl[r] for r in range(rows)], axis=1))
    own[2 * n + groups :, :] = jnp.exp(jnp.concatenate([hl[r] for r in range(rows)], axis=1))

    def pack(source, target):
        for z in range(ha):
            for r in range(rows):
                v = source[r, :, z * lanes : (z + 1) * lanes].astype(F32)
                a, b = cross(v[: cols // 2], v[cols // 2 :])
                target[z * pair, r] = a
                target[z * pair + 1, r] = b

    loads[4].wait()
    pack(cot_in, msg_c)

    pl.semaphore_wait(barrier, owners + chips - 2)
    sends = []
    made_small = []
    for d in range(1, ha):
        z = lax.rem(me_z + d, ha)
        made_small.append(remote(own, own, s_small.at[d], r_small.at[d], {"ha": z}))
    for c in made_small:
        c.start()

    def spread(k, message, landing):
        made = []
        for d in sorted(range(1, owners), key=lambda d: abs(d - owners // 2)):
            q = lax.rem(me_q + d, owners)
            made.append(remote(message.at[q], landing.at[me_q], s_in.at[k, q], r_in.at[k, me_q], column(q)))
        for c in made:
            c.start()
        landing[me_q] = message[me_q]
        sends.extend(made)

    def gather_in(k, z, message, landing, target):
        for e in range(pair):
            q = z * pair + e

            @pl.when(q != me_q)
            def _():
                remote(message.at[q], landing.at[q], s_in.at[k, q], r_in.at[k, q], column(q)).wait_recv()

        for r in range(rows):
            a, b = cross(landing[z * pair, r], landing[z * pair + 1, r])
            target[z * rows + r, 0 : cols // 2, :] = a
            target[z * rows + r, cols // 2 :, :] = b

    def arrive(made):
        for c in made:
            c.wait_recv()

    spread(0, msg_c, land_c)
    loads[5].wait()
    pack(tok_in, msg_x)
    spread(1, msg_x, land_x)

    l = lax.broadcasted_iota(jnp.int32, (lanes, pair * tokens), 0)
    o = lax.broadcasted_iota(jnp.int32, (lanes, pair * tokens), 1)
    column_of = jnp.where(lax.div(o, tokens) == lax.div(l, share), lax.rem(o, cols), -1)

    def place_tile(j, unused):
        ones = jnp.where(column_of == j, 1.0, 0.0).astype(BF16)
        place[pl.ds(pl.multiple_of(j * lanes, lanes), lanes), :] = ones
        return unused

    lax.fori_loop(0, cols, place_tile, 0)
    hold[...] = jnp.zeros_like(hold)
    total[...] = jnp.zeros_like(total)

    arrive(made_small)
    made_core = []
    for e in range(1, pair):
        c = lax.rem(core + e, pair)
        made_core.append(
            remote(small.at[core], small.at[core], s_core.at[e], r_core.at[e], {"wa": chip * pair + c})
        )
    for c in made_core:
        c.start()
    arrive(made_core)
    sends.extend(made_small)
    sends.extend(made_core)

    at = lax.broadcasted_iota(jnp.int32, (pair * groups, lanes), 0)
    lane = lax.broadcasted_iota(jnp.int32, (pair * groups, lanes), 1)
    pick = jnp.where(at == lax.div(lane, share) * groups + mine, 1.0, 0.0).astype(F32)
    for target, first in ((wr, 2 * n), (hr, 2 * n + groups)):
        for z in range(ha):
            rates = jnp.concatenate([small[c, z, first : first + groups, :] for c in range(pair)], axis=0)
            target[z * rows : (z + 1) * rows] = dot(rates, pick, ((0,), (0,))).reshape(rows, cols, lanes)

    def products(z, unused):
        rates = []
        for r in range(rows):
            i = z * rows + r
            one = wr[i]
            size = cols
            while size > 8:
                size //= 2
                one = one[:size] * one[size:]
            while size > 1:
                size //= 2
                one = one * pltpu.roll(one, size, 0)
            pw[i] = one[0:1]
            rates.append(one[0:1] * swap(one)[0:1])
        for p in range(rows // 2):
            pc_msg[z * (rows // 2) + p] = jnp.where(low((1, lanes)), rates[2 * p], rates[2 * p + 1])
        return unused

    lax.fori_loop(0, ha, products, 0)
    made_pc = []
    for d in range(1, chips):
        c = lax.rem(chip + d, chips)
        made_pc.append(remote(pc_msg, pc_land.at[chip], s_pc.at[d], r_pc.at[d], across(c)))
    for c in made_pc:
        c.start()
    sends.extend(made_pc)

    keep = low((n, lanes))

    def widen(first, target):
        def one(z, unused):
            left = small[0, z, first : first + n, :]
            right = small[1, z, first : first + n, :]
            for t in range(tokens):
                target[z * rows + t // cols, t % cols] = jnp.where(
                    keep,
                    jnp.broadcast_to(left[:, t : t + 1], (n, lanes)),
                    jnp.broadcast_to(right[:, t : t + 1], (n, lanes)),
                )
            return unused

        return one

    lax.fori_loop(0, ha, widen(0, cb), 0)
    lax.fori_loop(0, ha // 4, widen(n, bb), 0)

    def wide_copy(k, z, message, landing, source, to):
        return remote(
            message.at[z], landing.at[source, z], s_wide.at[k, z, to], r_wide.at[k, z, source], across(to)
        )

    def wide_send(k, z, message, landing, backward):
        for c in range(chips):

            @pl.when(c < chip if backward else c > chip)
            def _():
                wide_copy(k, z, message, landing, chip, c).start()

    def wide_done(k, z, message, landing, backward):
        for c in range(chips):

            @pl.when(c < chip if backward else c > chip)
            def _():
                wide_copy(k, z, message, landing, chip, c).wait_send()

    def wide_arrive(k, z, message, landing, backward):
        for c in range(chips):

            @pl.when(c > chip if backward else c < chip)
            def _():
                wide_copy(k, z, message, landing, c, c).wait_recv()

    def join(z, ends, message, backward):
        for p in range(rows // 2):
            i = z * rows + 2 * p
            a = ends[i] + pw[i] * swap(ends[i])
            b = ends[i + 1] + pw[i + 1] * swap(ends[i + 1])
            message[z, p] = jnp.where(keep, a, swap(b)) if backward else jnp.where(keep, swap(a), b)

    def enter(z, ends, landing, target, backward):
        def step(t, carry):
            c = chips - 1 - t if backward else t
            return tuple(
                pc_land[c, z * (rows // 2) + p] * carry[p] + landing[c, z, p] for p in range(rows // 2)
            )

        zero = jnp.zeros((n, lanes), F32)
        carry = lax.fori_loop(0, chips - 1 - chip if backward else chip, step, (zero,) * (rows // 2))
        for p in range(rows // 2):
            for s in range(2):
                i = z * rows + 2 * p + s
                k = swap(carry[p]) if (s == 0) == backward else carry[p]
                after = swap(ends[i] + pw[i] * k)
                target[i] = jnp.where(keep, after, k) if backward else jnp.where(keep, k, after)

    def col_scan(c, unused):
        z = ha - 1 - c
        gather_in(0, z, msg_c, land_c, cot)

        def one(t, unused):
            i = z * rows + rows - 1 - t
            carry = jnp.zeros((n, lanes), F32)
            for j in range(cols - 1, -1, -1):
                grad = cb[i, j] * cot[i, j : j + 1, :] + hold[j]
                grads[i, j] = grad
                hold[j] = hr[i, j : j + 1, :] * grad
                carry = wr[i, j : j + 1, :] * (grad + carry)
            ends_b[i] = carry
            return unused

        lax.fori_loop(0, rows, one, 0, unroll=True)
        join(z, ends_b, wb_msg, True)
        wide_send(0, z, wb_msg, wb_land, True)
        return unused

    lax.fori_loop(0, ha, col_scan, 0)
    lax.fori_loop(ha // 4, ha, widen(n, bb), 0)
    arrive(made_pc)

    def row_scan(c, unused):
        z = lax.rem(me_z + c, ha)
        gather_in(1, z, msg_x, land_x, x)

        def one(r, unused):
            i = z * rows + r
            carry = bb[i, 0] * x[i, 0:1, :]
            for j in range(1, cols):
                carry = wr[i, j : j + 1, :] * carry + bb[i, j] * x[i, j : j + 1, :]
            ends_f[i] = carry
            return unused

        lax.fori_loop(0, rows, one, 0, unroll=True)
        join(z, ends_f, wf_msg, False)
        wide_send(1, z, wf_msg, wf_land, False)
        return unused

    lax.fori_loop(0, ha, row_scan, 0)

    def keep_product(kept, r, j, v):
        top = v.astype(BF16)
        kept[r, 0:n, j * lanes : (j + 1) * lanes] = top
        kept[r, n:, j * lanes : (j + 1) * lanes] = (v - top.astype(F32)).astype(BF16)

    row_of = lax.div(lax.broadcasted_iota(jnp.int32, (n, tokens), 1), cols)

    def channel_sums(kept, message, z):
        v = jnp.dot(kept.reshape(rows * 2 * n, cols * lanes), place[...], preferred_element_type=F32)
        for e in range(pair):
            out = jnp.zeros((n, tokens), F32)
            for r in range(rows):
                part = v[r * 2 * n : (r + 1) * 2 * n, e * tokens : (e + 1) * tokens]
                out = jnp.where(row_of == r, part[:n] + part[n:], out)
            message[z * pair + e, 0:n] = out

    def group_sums():
        both = jnp.concatenate([part_w[...], part_h[...]], axis=0)
        top = both.astype(BF16)
        rest = (both - top.astype(F32)).astype(BF16)
        v = jnp.dot(jnp.concatenate([top, rest], axis=0), place[...], preferred_element_type=F32)
        v = v[: 2 * rows] + v[2 * rows :]
        sub = lax.broadcasted_iota(jnp.int32, (rows, tokens), 0)
        row = lax.div(lax.broadcasted_iota(jnp.int32, (rows, tokens), 1), cols)
        out = []
        for e in range(pair):
            part = v[:, e * tokens : (e + 1) * tokens]
            out.append(
                [
                    jnp.sum(jnp.where(sub == row, part[k * rows : (k + 1) * rows], 0.0), axis=0, keepdims=True)
                    for k in range(2)
                ]
            )
        return out

    def home(k, z, e, message, landing):
        q = z * pair + e
        return remote(message.at[q], landing.at[me_q], s_out.at[k, q], r_out.at[k, me_q], column(q))

    def go_home(k, z, message, landing):
        for e in range(pair):

            @pl.when(z * pair + e != me_q)
            def _():
                home(k, z, e, message, landing).start()

            @pl.when(z * pair + e == me_q)
            def _():
                pltpu.make_async_copy(message.at[me_q], landing.at[me_q], s_own.at[k]).start()

    def rows_done(c, unused):
        z = lax.rem(me_z + ha // 2 + c, ha)
        wide_arrive(0, z, wb_msg, wb_land, True)
        enter(z, ends_b, wb_land, cin_b, True)

        def one(r, unused):
            i = z * rows + r
            carry = cin_b[i]
            for j in range(cols - 1, -1, -1):
                grad = grads[i, j] + carry
                rows_grad[i, j] = grad
                carry = wr[i, j : j + 1, :] * grad
                tok_rows[r, j : j + 1, :] = jnp.sum(grad * bb[i, j], axis=0, keepdims=True)
                keep_product(prod_in, i, j, grad * x[i, j : j + 1, :])
            return unused

        lax.fori_loop(0, rows, one, 0, unroll=True)
        for r in range(rows):
            a, b = cross(tok_rows[r, 0 : cols // 2, :], tok_rows[r, cols // 2 :, :])
            tok_msg[z * pair, r] = a
            tok_msg[z * pair + 1, r] = b
        go_home(0, z, tok_msg, tok_home)
        channel_sums(prod_in[pl.ds(z * rows, rows)], in_msg, z)
        go_home(1, z, in_msg, in_home)
        return unused

    lax.fori_loop(0, ha, rows_done, 0)

    sub = lax.broadcasted_iota(jnp.int32, (8, tokens), 0)

    def cols_done(z, unused):
        wide_arrive(1, z, wf_msg, wf_land, False)
        enter(z, ends_f, wf_land, cin_f, False)

        def one(r, unused):
            i = z * rows + r
            carry = cin_f[i]
            for j in range(cols):
                w = rows_grad[i, j] * carry
                carry = wr[i, j : j + 1, :] * carry + bb[i, j] * x[i, j : j + 1, :]
                before = total[j]
                h = grads[i, j] * before
                now = hr[i, j : j + 1, :] * before + carry
                total[j] = now
                keep_product(prod, r, j, now * cot[i, j : j + 1, :])
                part_w[pl.ds(r, 1), j * lanes : (j + 1) * lanes] = jnp.sum(w, axis=0, keepdims=True)
                part_h[pl.ds(r, 1), j * lanes : (j + 1) * lanes] = jnp.sum(h, axis=0, keepdims=True)
            return unused

        lax.fori_loop(0, rows, one, 0, unroll=True)
        channel_sums(prod[...], fin_msg, z)
        for e, (w, h) in enumerate(group_sums()):
            fin_msg[z * pair + e, n:] = jnp.where(sub == 0, w, jnp.where(sub == 1, h, 0.0))
        go_home(2, z, fin_msg, fin_home)
        return unused

    lax.fori_loop(0, ha, cols_done, 0)

    for c in sends:
        c.wait_send()

    homes = ((0, tok_msg, tok_home), (1, in_msg, in_home), (2, fin_msg, fin_home))

    def sent(z, unused):
        wide_done(0, z, wb_msg, wb_land, True)
        wide_done(1, z, wf_msg, wf_land, False)
        for k, message, landing in homes:
            for e in range(pair):

                @pl.when(z * pair + e != me_q)
                def _():
                    home(k, z, e, message, landing).wait_send()

        return unused

    lax.fori_loop(0, ha, sent, 0)
    for k, message, landing in homes:
        for d in range(1, owners):
            q = lax.rem(me_q + d, owners)
            remote(message.at[q], landing.at[q], s_out.at[k, q], r_out.at[k, q], column(q)).wait_recv()
    for k, message, landing in ((0, tok_msg, tok_home), (1, in_msg, in_home), (2, fin_msg, fin_home)):
        pltpu.make_async_copy(message.at[me_q], landing.at[me_q], s_own.at[k]).wait()


def at_home(ha, pair, tok_home, in_home, fin_home, wl, hl, tok_out, in_out, so_out, wg_out, hg_out):
    rows, cols, channels = tok_out.shape
    n = in_out.shape[1]
    groups = wl.shape[1]
    lanes = channels // ha
    owners = ha * pair
    tokens = rows * cols
    for z in range(ha):
        for r in range(rows):
            a, b = cross(tok_home[z * pair, r], tok_home[z * pair + 1, r])
            tok_out[r, 0 : cols // 2, z * lanes : (z + 1) * lanes] = a
            tok_out[r, cols // 2 :, z * lanes : (z + 1) * lanes] = b
    in_sum, so_sum = in_home[0], fin_home[0, 0:n]
    for q in range(1, owners):
        in_sum = in_sum + in_home[q]
        so_sum = so_sum + fin_home[q, 0:n]
    in_out[...] = in_sum.T
    so_out[...] = so_sum.T
    sub = lax.broadcasted_iota(jnp.int32, (groups, tokens), 0)
    for k, decay, out in ((0, wl, wg_out), (1, hl, hg_out)):
        rate_sum = jnp.zeros((groups, tokens), F32)
        for q in range(owners):
            g = q * groups // owners
            rate_sum = rate_sum + jnp.where(sub == g, fin_home[q, n + k : n + k + 1, :], 0.0)
        for r in range(rows):
            out[r] = rate_sum[:, r * cols : (r + 1) * cols] * jnp.exp(decay[r])


def per_device(ha, wa, tokens, cotangent, state_in, state_out, width_decay, height_decay):
    rows, cols, channels = tokens.shape
    n = state_in.shape[2]
    groups = width_decay.shape[2]
    pair = 2
    chips = wa // pair
    owners = ha * pair
    lanes = channels // ha
    high = ha * rows
    count = rows * cols
    vmem = pl.BlockSpec(memory_space=pltpu.VMEM)
    far = pl.BlockSpec(memory_space=pl.ANY)
    room = lambda *shape: pltpu.VMEM(shape, F32)
    sems = lambda *shape: pltpu.SemaphoreType.DMA(shape)
    wl = jnp.swapaxes(width_decay, 1, 2)
    hl = jnp.swapaxes(height_decay, 1, 2)
    message = (owners, rows, cols // 2, lanes)
    state = (high, cols, n, lanes)
    ends = (high, n, lanes)
    wide = (ha, rows // 2, n, lanes)
    homes = pl.pallas_call(
        functools.partial(exchange, ha, chips, pair),
        out_shape=[
            jax.ShapeDtypeStruct(message, F32),
            jax.ShapeDtypeStruct((owners, n, count), F32),
            jax.ShapeDtypeStruct((owners, n + 8, count), F32),
        ],
        in_specs=[far] * 6,
        out_specs=[far] * 3,
        scratch_shapes=[
            pltpu.VMEM(tokens.shape, tokens.dtype),
            pltpu.VMEM(cotangent.shape, cotangent.dtype),
            room(*state_in.shape),
            room(*state_out.shape),
            room(*wl.shape),
            room(*hl.shape),
        ]
        + [room(*message) for _ in range(4)]
        + [room(pair, ha, 2 * n + 2 * groups, count)]
        + [room(high, cols, lanes) for _ in range(4)]
        + [room(*state) for _ in range(4)]
        + [room(cols, n, lanes) for _ in range(2)]
        + [room(*ends) for _ in range(4)]
        + [room(high, 1, lanes), room(high // 2, 1, lanes), room(chips, high // 2, 1, lanes)]
        + [room(*wide), room(chips, *wide), room(*wide), room(chips, *wide)]
        + [
            pltpu.VMEM((cols * lanes, pair * count), BF16),
            pltpu.VMEM((high, 2 * n, cols * lanes), BF16),
            pltpu.VMEM((rows, 2 * n, cols * lanes), BF16),
            room(rows, cols * lanes),
            room(rows, cols * lanes),
            room(rows, cols, lanes),
            room(*message),
            room(owners, n, count),
            room(owners, n + 8, count),
        ]
        + [sems(ha), sems(ha), sems(pair), sems(pair)]
        + [sems(2, owners), sems(2, owners), sems(chips), sems(chips)]
        + [sems(2, ha, chips), sems(2, ha, chips), sems(3, owners), sems(3, owners), sems(6), sems(3)],
        compiler_params=pltpu.CompilerParams(
            collective_id=0, has_side_effects=True, vmem_limit_bytes=56 * 1024 * 1024
        ),
        name="exchange",
    )(tokens, cotangent, state_in, state_out, wl, hl)
    result = pl.pallas_call(
        functools.partial(at_home, ha, pair),
        out_shape=[
            jax.ShapeDtypeStruct((rows, cols, channels), F32),
            jax.ShapeDtypeStruct((count, n), F32),
            jax.ShapeDtypeStruct((count, n), F32),
            jax.ShapeDtypeStruct((rows, groups, cols), F32),
            jax.ShapeDtypeStruct((rows, groups, cols), F32),
        ],
        in_specs=[vmem] * 5,
        out_specs=[vmem] * 5,
        name="at_home",
    )(*homes, wl, hl)
    return (
        result[0],
        result[1].reshape(rows, cols, n),
        result[2].reshape(rows, cols, n),
        jnp.swapaxes(result[3], 1, 2),
        jnp.swapaxes(result[4], 1, 2),
    )


def solution(mesh):
    spec = P("ha", "wa", None)
    return jax.shard_map(
        functools.partial(per_device, mesh.shape["ha"], mesh.shape["wa"]),
        mesh=mesh,
        in_specs=(spec,) * 6,
        out_specs=(spec,) * 5,
        check_vma=False,
    )
```

```python
import functools

import jax
import jax.numpy as jnp
from jax import lax
from jax.experimental import pallas as pl
from jax.experimental.pallas import tpu as pltpu
from jax.sharding import PartitionSpec as P

MESH = pl.DeviceIdType.MESH
F32 = jnp.float32
BF16 = jnp.bfloat16
HIGHEST = lax.Precision.HIGHEST


def swap(v):
    half = v.shape[-1] // 2
    if v.shape[-1] % 128 == 0:
        return pltpu.roll(v, half, v.ndim - 1)
    return jnp.concatenate([v[..., half:], v[..., :half]], axis=-1)


def low(shape):
    return lax.broadcasted_iota(jnp.int32, shape, len(shape) - 1) < shape[-1] // 2


def cross(a, b):
    keep = low(a.shape)
    return jnp.where(keep, a, swap(b)), jnp.where(keep, swap(a), b)


def exchange(
    ha,
    chips,
    pair,
    tok_far,
    cot_far,
    b_far,
    c_far,
    wl_far,
    hl_far,
    tok_home,
    in_home,
    fin_home,
    tok_in,
    cot_in,
    b_in,
    c_in,
    wl,
    hl,
    msg_c,
    msg_x,
    land_c,
    land_x,
    small,
    cot,
    x,
    wr,
    hr,
    cb,
    bb,
    grads,
    rows_grad,
    hold,
    total,
    ends_b,
    ends_f,
    cin_b,
    cin_f,
    pw,
    pc_msg,
    pc_land,
    wb_msg,
    wb_land,
    wf_msg,
    wf_land,
    place,
    prod_in,
    prod,
    part_w,
    part_h,
    tok_rows,
    tok_msg,
    in_msg,
    fin_msg,
    s_small,
    r_small,
    s_core,
    r_core,
    s_in,
    r_in,
    s_pc,
    r_pc,
    s_wide,
    r_wide,
    s_out,
    r_out,
    s_load,
    s_own,
):
    rows, cols, channels = tok_in.shape
    n = b_in.shape[2]
    groups = wl.shape[1]
    lanes = channels // ha
    share = lanes // pair
    owners = ha * pair
    high = ha * rows
    tokens = rows * cols
    me_z = lax.axis_index("ha")
    me_w = lax.axis_index("wa")
    chip = me_w // pair
    core = lax.rem(me_w, pair)
    me_q = me_z * pair + core
    mine = lax.div(me_q * share, channels // groups)

    def column(q):
        return {"ha": lax.div(q, pair), "wa": chip * pair + lax.rem(q, pair)}

    def across(c):
        return {"wa": c * pair + core}

    def remote(src, dst, ss, rs, device):
        return pltpu.make_async_remote_copy(
            src_ref=src, dst_ref=dst, send_sem=ss, recv_sem=rs, device_id=device, device_id_type=MESH
        )

    def dot(a, b, dims):
        return lax.dot_general(a, b, (dims, ((), ())), precision=HIGHEST, preferred_element_type=F32)

    barrier = pltpu.get_barrier_semaphore()
    for d in range(1, owners):
        pl.semaphore_signal(
            barrier, inc=1, device_id=column(lax.rem(me_q + d, owners)), device_id_type=MESH
        )
    for d in range(1, chips):
        pl.semaphore_signal(
            barrier, inc=1, device_id=across(lax.rem(chip + d, chips)), device_id_type=MESH
        )

    loads = [
        pltpu.make_async_copy(far, near, s_load.at[k])
        for k, (far, near) in enumerate(
            ((c_far, c_in), (b_far, b_in), (wl_far, wl), (hl_far, hl), (cot_far, cot_in), (tok_far, tok_in))
        )
    ]
    for c in loads:
        c.start()
    for c in loads[:4]:
        c.wait()

    eye = jnp.where(
        lax.broadcasted_iota(jnp.int32, (n, n), 0) == lax.broadcasted_iota(jnp.int32, (n, n), 1), 1.0, 0.0
    ).astype(F32)
    own = small.at[core, me_z]
    own[0:n, :] = dot(eye, c_in[...].reshape(tokens, n), ((1,), (1,)))
    own[n : 2 * n, :] = dot(eye, b_in[...].reshape(tokens, n), ((1,), (1,)))
    own[2 * n : 2 * n + groups, :] = jnp.exp(jnp.concatenate([wl[r] for r in range(rows)], axis=1))
    own[2 * n + groups :, :] = jnp.exp(jnp.concatenate([hl[r] for r in range(rows)], axis=1))

    def pack(source, target):
        for z in range(ha):
            for r in range(rows):
                v = source[r, :, z * lanes : (z + 1) * lanes].astype(F32)
                a, b = cross(v[: cols // 2], v[cols // 2 :])
                target[z * pair, r] = a
                target[z * pair + 1, r] = b

    loads[4].wait()
    pack(cot_in, msg_c)

    pl.semaphore_wait(barrier, owners + chips - 2)
    sends = []
    made_small = []
    for d in range(1, ha):
        z = lax.rem(me_z + d, ha)
        made_small.append(remote(own, own, s_small.at[d], r_small.at[d], {"ha": z}))
    made_core = []
    for d in range(ha):
        z = lax.rem(me_z + ha - d, ha)
        for e in range(1, pair):
            c = lax.rem(core + e, pair)
            made_core.append(
                remote(
                    small.at[core, z], small.at[core, z], s_core.at[e, d], r_core.at[e, d], {"wa": chip * pair + c}
                )
            )
    for c in made_small + made_core[: pair - 1]:
        c.start()

    def spread(k, message, landing):
        made = []
        for d in sorted(range(1, owners), key=lambda d: abs(d - owners // 2)):
            q = lax.rem(me_q + d, owners)
            made.append(remote(message.at[q], landing.at[me_q], s_in.at[k, q], r_in.at[k, me_q], column(q)))
        for c in made:
            c.start()
        landing[me_q] = message[me_q]
        sends.extend(made)

    def gather_in(k, z, message, landing, target):
        for e in range(pair):
            q = z * pair + e

            @pl.when(q != me_q)
            def _():
                remote(message.at[q], landing.at[q], s_in.at[k, q], r_in.at[k, q], column(q)).wait_recv()

        for r in range(rows):
            a, b = cross(landing[z * pair, r], landing[z * pair + 1, r])
            target[z * rows + r, 0 : cols // 2, :] = a
            target[z * rows + r, cols // 2 :, :] = b

    def arrive(made):
        for c in made:
            c.wait_recv()

    spread(0, msg_c, land_c)
    loads[5].wait()
    pack(tok_in, msg_x)
    spread(1, msg_x, land_x)

    l = lax.broadcasted_iota(jnp.int32, (lanes, pair * tokens), 0)
    o = lax.broadcasted_iota(jnp.int32, (lanes, pair * tokens), 1)
    column_of = jnp.where(lax.div(o, tokens) == lax.div(l, share), lax.rem(o, cols), -1)

    def place_tile(j, unused):
        ones = jnp.where(column_of == j, 1.0, 0.0).astype(BF16)
        place[pl.ds(pl.multiple_of(j * lanes, lanes), lanes), :] = ones
        return unused

    lax.fori_loop(0, cols, place_tile, 0)
    hold[...] = jnp.zeros_like(hold)
    total[...] = jnp.zeros_like(total)

    keep = low((n, lanes))

    def widen(first, target):
        def one(k, unused):
            z = lax.rem(me_z + k, ha)
            left = small[0, z, first : first + n, :]
            right = small[1, z, first : first + n, :]
            for t in range(tokens):
                target[z * rows + t // cols, t % cols] = jnp.where(
                    keep,
                    jnp.broadcast_to(left[:, t : t + 1], (n, lanes)),
                    jnp.broadcast_to(right[:, t : t + 1], (n, lanes)),
                )
            return unused

        return one

    arrive(made_core[: pair - 1])
    lax.fori_loop(0, 1, widen(0, cb), 0)
    lax.fori_loop(0, 1, widen(n, bb), 0)
    for d in range(1, ha):
        made_small[d - 1].wait_recv()
        for c in made_core[d * (pair - 1) : (d + 1) * (pair - 1)]:
            c.start()
    arrive(made_core[pair - 1 :])
    sends.extend(made_small)
    sends.extend(made_core)

    at = lax.broadcasted_iota(jnp.int32, (pair * groups, lanes), 0)
    lane = lax.broadcasted_iota(jnp.int32, (pair * groups, lanes), 1)
    pick = jnp.where(at == lax.div(lane, share) * groups + mine, 1.0, 0.0).astype(F32)
    for target, first in ((wr, 2 * n), (hr, 2 * n + groups)):
        for z in range(ha):
            rates = jnp.concatenate([small[c, z, first : first + groups, :] for c in range(pair)], axis=0)
            target[z * rows : (z + 1) * rows] = dot(rates, pick, ((0,), (0,))).reshape(rows, cols, lanes)

    def products(z, unused):
        rates = []
        for r in range(rows):
            i = z * rows + r
            one = wr[i]
            size = cols
            while size > 8:
                size //= 2
                one = one[:size] * one[size:]
            while size > 1:
                size //= 2
                one = one * pltpu.roll(one, size, 0)
            pw[i] = one[0:1]
            rates.append(one[0:1] * swap(one)[0:1])
        for p in range(rows // 2):
            pc_msg[z * (rows // 2) + p] = jnp.where(low((1, lanes)), rates[2 * p], rates[2 * p + 1])
        return unused

    lax.fori_loop(0, ha, products, 0)
    made_pc = []
    for d in range(1, chips):
        c = lax.rem(chip + d, chips)
        made_pc.append(remote(pc_msg, pc_land.at[chip], s_pc.at[d], r_pc.at[d], across(c)))
    for c in made_pc:
        c.start()
    sends.extend(made_pc)

    lax.fori_loop(1, ha, widen(0, cb), 0)
    lax.fori_loop(1, 2, widen(n, bb), 0)

    def wide_copy(k, z, message, landing, source, to):
        return remote(
            message.at[z], landing.at[source, z], s_wide.at[k, z, to], r_wide.at[k, z, source], across(to)
        )

    def wide_send(k, z, message, landing, backward):
        for c in range(chips):

            @pl.when(c < chip if backward else c > chip)
            def _():
                wide_copy(k, z, message, landing, chip, c).start()

    def wide_done(k, z, message, landing, backward):
        for c in range(chips):

            @pl.when(c < chip if backward else c > chip)
            def _():
                wide_copy(k, z, message, landing, chip, c).wait_send()

    def wide_arrive(k, z, message, landing, backward):
        for c in range(chips):

            @pl.when(c > chip if backward else c < chip)
            def _():
                wide_copy(k, z, message, landing, c, c).wait_recv()

    def join(z, ends, message, backward):
        for p in range(rows // 2):
            i = z * rows + 2 * p
            a = ends[i] + pw[i] * swap(ends[i])
            b = ends[i + 1] + pw[i + 1] * swap(ends[i + 1])
            message[z, p] = jnp.where(keep, a, swap(b)) if backward else jnp.where(keep, swap(a), b)

    def enter(z, ends, landing, target, backward):
        def step(t, carry):
            c = chips - 1 - t if backward else t
            return tuple(
                pc_land[c, z * (rows // 2) + p] * carry[p] + landing[c, z, p] for p in range(rows // 2)
            )

        zero = jnp.zeros((n, lanes), F32)
        carry = lax.fori_loop(0, chips - 1 - chip if backward else chip, step, (zero,) * (rows // 2))
        for p in range(rows // 2):
            for s in range(2):
                i = z * rows + 2 * p + s
                k = swap(carry[p]) if (s == 0) == backward else carry[p]
                after = swap(ends[i] + pw[i] * k)
                target[i] = jnp.where(keep, after, k) if backward else jnp.where(keep, k, after)

    def col_scan(c, unused):
        z = ha - 1 - c
        gather_in(0, z, msg_c, land_c, cot)

        def one(t, unused):
            i = z * rows + rows - 1 - t
            carry = jnp.zeros((n, lanes), F32)
            for j in range(cols - 1, -1, -1):
                grad = cb[i, j] * cot[i, j : j + 1, :] + hold[j]
                grads[i, j] = grad
                hold[j] = hr[i, j : j + 1, :] * grad
                carry = wr[i, j : j + 1, :] * (grad + carry)
            ends_b[i] = carry
            return unused

        lax.fori_loop(0, rows, one, 0, unroll=True)
        join(z, ends_b, wb_msg, True)
        wide_send(0, z, wb_msg, wb_land, True)
        return unused

    lax.fori_loop(0, ha, col_scan, 0)
    lax.fori_loop(2, ha, widen(n, bb), 0)
    arrive(made_pc)

    def row_scan(c, unused):
        z = lax.rem(me_z + c, ha)
        gather_in(1, z, msg_x, land_x, x)

        def one(r, unused):
            i = z * rows + r
            carry = bb[i, 0] * x[i, 0:1, :]
            for j in range(1, cols):
                carry = wr[i, j : j + 1, :] * carry + bb[i, j] * x[i, j : j + 1, :]
            ends_f[i] = carry
            return unused

        lax.fori_loop(0, rows, one, 0, unroll=True)
        join(z, ends_f, wf_msg, False)
        wide_send(1, z, wf_msg, wf_land, False)
        return unused

    lax.fori_loop(0, ha, row_scan, 0)

    def keep_product(kept, r, j, v):
        top = v.astype(BF16)
        kept[r, 0:n, j * lanes : (j + 1) * lanes] = top
        kept[r, n:, j * lanes : (j + 1) * lanes] = (v - top.astype(F32)).astype(BF16)

    row_of = lax.div(lax.broadcasted_iota(jnp.int32, (n, tokens), 1), cols)

    def channel_sums(kept, message, z):
        v = jnp.dot(kept.reshape(rows * 2 * n, cols * lanes), place[...], preferred_element_type=F32)
        for e in range(pair):
            out = jnp.zeros((n, tokens), F32)
            for r in range(rows):
                part = v[r * 2 * n : (r + 1) * 2 * n, e * tokens : (e + 1) * tokens]
                out = jnp.where(row_of == r, part[:n] + part[n:], out)
            message[z * pair + e, 0:n] = out

    def group_sums():
        both = jnp.concatenate([part_w[...], part_h[...]], axis=0)
        top = both.astype(BF16)
        rest = (both - top.astype(F32)).astype(BF16)
        v = jnp.dot(jnp.concatenate([top, rest], axis=0), place[...], preferred_element_type=F32)
        v = v[: 2 * rows] + v[2 * rows :]
        sub = lax.broadcasted_iota(jnp.int32, (rows, tokens), 0)
        row = lax.div(lax.broadcasted_iota(jnp.int32, (rows, tokens), 1), cols)
        out = []
        for e in range(pair):
            part = v[:, e * tokens : (e + 1) * tokens]
            out.append(
                [
                    jnp.sum(jnp.where(sub == row, part[k * rows : (k + 1) * rows], 0.0), axis=0, keepdims=True)
                    for k in range(2)
                ]
            )
        return out

    def home(k, z, e, message, landing):
        q = z * pair + e
        return remote(message.at[q], landing.at[me_q], s_out.at[k, q], r_out.at[k, me_q], column(q))

    def go_home(k, z, message, landing):
        for e in range(pair):

            @pl.when(z * pair + e != me_q)
            def _():
                home(k, z, e, message, landing).start()

            @pl.when(z * pair + e == me_q)
            def _():
                pltpu.make_async_copy(message.at[me_q], landing.at[me_q], s_own.at[k]).start()

    def rows_done(c, unused):
        z = lax.rem(me_z + ha // 2 + c, ha)
        wide_arrive(0, z, wb_msg, wb_land, True)
        enter(z, ends_b, wb_land, cin_b, True)

        def one(r, unused):
            i = z * rows + r
            carry = cin_b[i]
            for j in range(cols - 1, -1, -1):
                grad = grads[i, j] + carry
                rows_grad[i, j] = grad
                carry = wr[i, j : j + 1, :] * grad
                tok_rows[r, j : j + 1, :] = jnp.sum(grad * bb[i, j], axis=0, keepdims=True)
                keep_product(prod_in, i, j, grad * x[i, j : j + 1, :])
            return unused

        lax.fori_loop(0, rows, one, 0, unroll=True)
        for r in range(rows):
            a, b = cross(tok_rows[r, 0 : cols // 2, :], tok_rows[r, cols // 2 :, :])
            tok_msg[z * pair, r] = a
            tok_msg[z * pair + 1, r] = b
        go_home(0, z, tok_msg, tok_home)
        channel_sums(prod_in[pl.ds(z * rows, rows)], in_msg, z)
        go_home(1, z, in_msg, in_home)
        return unused

    lax.fori_loop(0, ha, rows_done, 0)

    sub = lax.broadcasted_iota(jnp.int32, (8, tokens), 0)

    def cols_done(z, unused):
        wide_arrive(1, z, wf_msg, wf_land, False)
        enter(z, ends_f, wf_land, cin_f, False)

        def one(r, unused):
            i = z * rows + r
            carry = cin_f[i]
            for j in range(cols):
                w = rows_grad[i, j] * carry
                carry = wr[i, j : j + 1, :] * carry + bb[i, j] * x[i, j : j + 1, :]
                before = total[j]
                h = grads[i, j] * before
                now = hr[i, j : j + 1, :] * before + carry
                total[j] = now
                keep_product(prod, r, j, now * cot[i, j : j + 1, :])
                part_w[pl.ds(r, 1), j * lanes : (j + 1) * lanes] = jnp.sum(w, axis=0, keepdims=True)
                part_h[pl.ds(r, 1), j * lanes : (j + 1) * lanes] = jnp.sum(h, axis=0, keepdims=True)
            return unused

        lax.fori_loop(0, rows, one, 0, unroll=True)
        channel_sums(prod[...], fin_msg, z)
        for e, (w, h) in enumerate(group_sums()):
            fin_msg[z * pair + e, n:] = jnp.where(sub == 0, w, jnp.where(sub == 1, h, 0.0))
        go_home(2, z, fin_msg, fin_home)
        return unused

    lax.fori_loop(0, ha, cols_done, 0)

    for c in sends:
        c.wait_send()

    homes = ((0, tok_msg, tok_home), (1, in_msg, in_home), (2, fin_msg, fin_home))

    def sent(z, unused):
        wide_done(0, z, wb_msg, wb_land, True)
        wide_done(1, z, wf_msg, wf_land, False)
        for k, message, landing in homes:
            for e in range(pair):

                @pl.when(z * pair + e != me_q)
                def _():
                    home(k, z, e, message, landing).wait_send()

        return unused

    lax.fori_loop(0, ha, sent, 0)
    for k, message, landing in homes:
        for d in range(1, owners):
            q = lax.rem(me_q + d, owners)
            remote(message.at[q], landing.at[q], s_out.at[k, q], r_out.at[k, q], column(q)).wait_recv()
    for k, message, landing in ((0, tok_msg, tok_home), (1, in_msg, in_home), (2, fin_msg, fin_home)):
        pltpu.make_async_copy(message.at[me_q], landing.at[me_q], s_own.at[k]).wait()


def at_home(ha, pair, tok_home, in_home, fin_home, wl, hl, tok_out, in_out, so_out, wg_out, hg_out):
    rows, cols, channels = tok_out.shape
    n = in_out.shape[1]
    groups = wl.shape[1]
    lanes = channels // ha
    owners = ha * pair
    tokens = rows * cols
    for z in range(ha):
        for r in range(rows):
            a, b = cross(tok_home[z * pair, r], tok_home[z * pair + 1, r])
            tok_out[r, 0 : cols // 2, z * lanes : (z + 1) * lanes] = a
            tok_out[r, cols // 2 :, z * lanes : (z + 1) * lanes] = b
    in_sum, so_sum = in_home[0], fin_home[0, 0:n]
    for q in range(1, owners):
        in_sum = in_sum + in_home[q]
        so_sum = so_sum + fin_home[q, 0:n]
    in_out[...] = in_sum.T
    so_out[...] = so_sum.T
    sub = lax.broadcasted_iota(jnp.int32, (groups, tokens), 0)
    for k, decay, out in ((0, wl, wg_out), (1, hl, hg_out)):
        rate_sum = jnp.zeros((groups, tokens), F32)
        for q in range(owners):
            g = q * groups // owners
            rate_sum = rate_sum + jnp.where(sub == g, fin_home[q, n + k : n + k + 1, :], 0.0)
        for r in range(rows):
            out[r] = rate_sum[:, r * cols : (r + 1) * cols] * jnp.exp(decay[r])


def per_device(ha, wa, tokens, cotangent, state_in, state_out, width_decay, height_decay):
    rows, cols, channels = tokens.shape
    n = state_in.shape[2]
    groups = width_decay.shape[2]
    pair = 2
    chips = wa // pair
    owners = ha * pair
    lanes = channels // ha
    high = ha * rows
    count = rows * cols
    vmem = pl.BlockSpec(memory_space=pltpu.VMEM)
    far = pl.BlockSpec(memory_space=pl.ANY)
    room = lambda *shape: pltpu.VMEM(shape, F32)
    sems = lambda *shape: pltpu.SemaphoreType.DMA(shape)
    wl = jnp.swapaxes(width_decay, 1, 2)
    hl = jnp.swapaxes(height_decay, 1, 2)
    message = (owners, rows, cols // 2, lanes)
    state = (high, cols, n, lanes)
    ends = (high, n, lanes)
    wide = (ha, rows // 2, n, lanes)
    homes = pl.pallas_call(
        functools.partial(exchange, ha, chips, pair),
        out_shape=[
            jax.ShapeDtypeStruct(message, F32),
            jax.ShapeDtypeStruct((owners, n, count), F32),
            jax.ShapeDtypeStruct((owners, n + 8, count), F32),
        ],
        in_specs=[far] * 6,
        out_specs=[far] * 3,
        scratch_shapes=[
            pltpu.VMEM(tokens.shape, tokens.dtype),
            pltpu.VMEM(cotangent.shape, cotangent.dtype),
            room(*state_in.shape),
            room(*state_out.shape),
            room(*wl.shape),
            room(*hl.shape),
        ]
        + [room(*message) for _ in range(4)]
        + [room(pair, ha, 2 * n + 2 * groups, count)]
        + [room(high, cols, lanes) for _ in range(4)]
        + [room(*state) for _ in range(4)]
        + [room(cols, n, lanes) for _ in range(2)]
        + [room(*ends) for _ in range(4)]
        + [room(high, 1, lanes), room(high // 2, 1, lanes), room(chips, high // 2, 1, lanes)]
        + [room(*wide), room(chips, *wide), room(*wide), room(chips, *wide)]
        + [
            pltpu.VMEM((cols * lanes, pair * count), BF16),
            pltpu.VMEM((high, 2 * n, cols * lanes), BF16),
            pltpu.VMEM((rows, 2 * n, cols * lanes), BF16),
            room(rows, cols * lanes),
            room(rows, cols * lanes),
            room(rows, cols, lanes),
            room(*message),
            room(owners, n, count),
            room(owners, n + 8, count),
        ]
        + [sems(ha), sems(ha), sems(pair, ha), sems(pair, ha)]
        + [sems(2, owners), sems(2, owners), sems(chips), sems(chips)]
        + [sems(2, ha, chips), sems(2, ha, chips), sems(3, owners), sems(3, owners), sems(6), sems(3)],
        compiler_params=pltpu.CompilerParams(
            collective_id=0, has_side_effects=True, vmem_limit_bytes=56 * 1024 * 1024
        ),
        name="exchange",
    )(tokens, cotangent, state_in, state_out, wl, hl)
    result = pl.pallas_call(
        functools.partial(at_home, ha, pair),
        out_shape=[
            jax.ShapeDtypeStruct((rows, cols, channels), F32),
            jax.ShapeDtypeStruct((count, n), F32),
            jax.ShapeDtypeStruct((count, n), F32),
            jax.ShapeDtypeStruct((rows, groups, cols), F32),
            jax.ShapeDtypeStruct((rows, groups, cols), F32),
        ],
        in_specs=[vmem] * 5,
        out_specs=[vmem] * 5,
        name="at_home",
    )(*homes, wl, hl)
    return (
        result[0],
        result[1].reshape(rows, cols, n),
        result[2].reshape(rows, cols, n),
        jnp.swapaxes(result[3], 1, 2),
        jnp.swapaxes(result[4], 1, 2),
    )


def solution(mesh):
    spec = P("ha", "wa", None)
    return jax.shard_map(
        functools.partial(per_device, mesh.shape["ha"], mesh.shape["wa"]),
        mesh=mesh,
        in_specs=(spec,) * 6,
        out_specs=(spec,) * 5,
        check_vma=False,
    )
```

```python
import functools

import jax
import jax.numpy as jnp
from jax import lax
from jax.experimental import pallas as pl
from jax.experimental.pallas import tpu as pltpu
from jax.sharding import PartitionSpec as P

MESH = pl.DeviceIdType.MESH
F32 = jnp.float32
BF16 = jnp.bfloat16
HIGHEST = lax.Precision.HIGHEST


def swap(v):
    half = v.shape[-1] // 2
    if v.shape[-1] % 128 == 0:
        return pltpu.roll(v, half, v.ndim - 1)
    return jnp.concatenate([v[..., half:], v[..., :half]], axis=-1)


def low(shape):
    return lax.broadcasted_iota(jnp.int32, shape, len(shape) - 1) < shape[-1] // 2


def cross(a, b):
    keep = low(a.shape)
    return jnp.where(keep, a, swap(b)), jnp.where(keep, swap(a), b)


def exchange(
    ha,
    chips,
    pair,
    tok_far,
    cot_far,
    b_far,
    c_far,
    wl_far,
    hl_far,
    tok_home,
    in_home,
    fin_home,
    tok_in,
    cot_in,
    b_in,
    c_in,
    wl,
    hl,
    msg_c,
    msg_x,
    land_c,
    land_x,
    small,
    cot,
    x,
    wr,
    hr,
    cb,
    bb,
    grads,
    rows_grad,
    hold,
    total,
    ends_b,
    ends_f,
    cin_b,
    cin_f,
    pw,
    pc_msg,
    pc_land,
    wb_msg,
    wb_land,
    wf_msg,
    wf_land,
    place,
    prod_in,
    prod,
    part_w,
    part_h,
    tok_rows,
    tok_msg,
    in_msg,
    fin_msg,
    s_small,
    r_small,
    s_core,
    r_core,
    s_in,
    r_in,
    s_pc,
    r_pc,
    s_wide,
    r_wide,
    s_out,
    r_out,
    s_load,
    s_own,
):
    rows, cols, channels = tok_in.shape
    n = b_in.shape[2]
    groups = wl.shape[1]
    lanes = channels // ha
    share = lanes // pair
    owners = ha * pair
    high = ha * rows
    tokens = rows * cols
    me_z = lax.axis_index("ha")
    me_w = lax.axis_index("wa")
    chip = me_w // pair
    core = lax.rem(me_w, pair)
    me_q = me_z * pair + core
    mine = lax.div(me_q * share, channels // groups)

    def column(q):
        return {"ha": lax.div(q, pair), "wa": chip * pair + lax.rem(q, pair)}

    def across(c):
        return {"wa": c * pair + core}

    def remote(src, dst, ss, rs, device):
        return pltpu.make_async_remote_copy(
            src_ref=src, dst_ref=dst, send_sem=ss, recv_sem=rs, device_id=device, device_id_type=MESH
        )

    def dot(a, b, dims):
        return lax.dot_general(a, b, (dims, ((), ())), precision=HIGHEST, preferred_element_type=F32)

    barrier = pltpu.get_barrier_semaphore()
    for d in range(1, owners):
        pl.semaphore_signal(
            barrier, inc=1, device_id=column(lax.rem(me_q + d, owners)), device_id_type=MESH
        )
    for d in range(1, chips):
        pl.semaphore_signal(
            barrier, inc=1, device_id=across(lax.rem(chip + d, chips)), device_id_type=MESH
        )

    loads = [
        pltpu.make_async_copy(far, near, s_load.at[k])
        for k, (far, near) in enumerate(
            ((c_far, c_in), (b_far, b_in), (wl_far, wl), (hl_far, hl), (cot_far, cot_in), (tok_far, tok_in))
        )
    ]
    for c in loads:
        c.start()
    for c in loads[:4]:
        c.wait()

    eye = jnp.where(
        lax.broadcasted_iota(jnp.int32, (n, n), 0) == lax.broadcasted_iota(jnp.int32, (n, n), 1), 1.0, 0.0
    ).astype(F32)
    own = small.at[core, me_z]
    own[0:n, :] = dot(eye, c_in[...].reshape(tokens, n), ((1,), (1,)))
    own[n : 2 * n, :] = dot(eye, b_in[...].reshape(tokens, n), ((1,), (1,)))
    own[2 * n : 2 * n + groups, :] = jnp.exp(jnp.concatenate([wl[r] for r in range(rows)], axis=1))
    own[2 * n + groups :, :] = jnp.exp(jnp.concatenate([hl[r] for r in range(rows)], axis=1))

    def pack(source, target):
        for z in range(ha):
            for r in range(rows):
                v = source[r, :, z * lanes : (z + 1) * lanes].astype(F32)
                a, b = cross(v[: cols // 2], v[cols // 2 :])
                target[z * pair, r] = a
                target[z * pair + 1, r] = b

    loads[4].wait()
    pack(cot_in, msg_c)

    pl.semaphore_wait(barrier, owners + chips - 2)
    sends = []
    made_small = []
    for d in range(1, ha):
        z = lax.rem(me_z + d, ha)
        made_small.append(remote(own, own, s_small.at[d], r_small.at[d], {"ha": z}))
    made_core = []
    for d in range(ha):
        z = lax.rem(me_z + ha - d, ha)
        for e in range(1, pair):
            c = lax.rem(core + e, pair)
            made_core.append(
                remote(
                    small.at[core, z], small.at[core, z], s_core.at[e, d], r_core.at[e, d], {"wa": chip * pair + c}
                )
            )
    for c in made_small + made_core[: pair - 1]:
        c.start()

    def spread(k, message, landing):
        made = []
        for d in sorted(range(1, owners), key=lambda d: abs(d - owners // 2)):
            q = lax.rem(me_q + d, owners)
            made.append(remote(message.at[q], landing.at[me_q], s_in.at[k, q], r_in.at[k, me_q], column(q)))
        for c in made:
            c.start()
        landing[me_q] = message[me_q]
        sends.extend(made)

    def gather_in(k, z, message, landing, target):
        for e in range(pair):
            q = z * pair + e

            @pl.when(q != me_q)
            def _():
                remote(message.at[q], landing.at[q], s_in.at[k, q], r_in.at[k, q], column(q)).wait_recv()

        for r in range(rows):
            a, b = cross(landing[z * pair, r], landing[z * pair + 1, r])
            target[z * rows + r, 0 : cols // 2, :] = a
            target[z * rows + r, cols // 2 :, :] = b

    def arrive(made):
        for c in made:
            c.wait_recv()

    spread(0, msg_c, land_c)
    loads[5].wait()
    pack(tok_in, msg_x)
    spread(1, msg_x, land_x)

    l = lax.broadcasted_iota(jnp.int32, (lanes, pair * tokens), 0)
    o = lax.broadcasted_iota(jnp.int32, (lanes, pair * tokens), 1)
    column_of = jnp.where(lax.div(o, tokens) == lax.div(l, share), lax.rem(o, cols), -1)

    def place_tile(j, unused):
        ones = jnp.where(column_of == j, 1.0, 0.0).astype(BF16)
        place[pl.ds(pl.multiple_of(j * lanes, lanes), lanes), :] = ones
        return unused

    lax.fori_loop(0, cols, place_tile, 0)
    hold[...] = jnp.zeros_like(hold)
    total[...] = jnp.zeros_like(total)

    keep = low((n, lanes))

    def widen(first, target):
        def one(k, unused):
            z = lax.rem(me_z + k, ha)
            left = small[0, z, first : first + n, :]
            right = small[1, z, first : first + n, :]
            for t in range(tokens):
                target[z * rows + t // cols, t % cols] = jnp.where(
                    keep,
                    jnp.broadcast_to(left[:, t : t + 1], (n, lanes)),
                    jnp.broadcast_to(right[:, t : t + 1], (n, lanes)),
                )
            return unused

        return one

    arrive(made_core[: pair - 1])
    lax.fori_loop(0, 1, widen(0, cb), 0)
    lax.fori_loop(0, 1, widen(n, bb), 0)
    for d in range(1, ha):
        made_small[d - 1].wait_recv()
        for c in made_core[d * (pair - 1) : (d + 1) * (pair - 1)]:
            c.start()
    for d in range(1, ha):
        arrive(made_core[d * (pair - 1) : (d + 1) * (pair - 1)])
        lax.fori_loop(ha - d, ha - d + 1, widen(0, cb), 0)
    sends.extend(made_small)
    sends.extend(made_core)

    at = lax.broadcasted_iota(jnp.int32, (pair * groups, lanes), 0)
    lane = lax.broadcasted_iota(jnp.int32, (pair * groups, lanes), 1)
    pick = jnp.where(at == lax.div(lane, share) * groups + mine, 1.0, 0.0).astype(F32)
    for target, first in ((wr, 2 * n), (hr, 2 * n + groups)):
        for z in range(ha):
            rates = jnp.concatenate([small[c, z, first : first + groups, :] for c in range(pair)], axis=0)
            target[z * rows : (z + 1) * rows] = dot(rates, pick, ((0,), (0,))).reshape(rows, cols, lanes)

    def products(z, unused):
        rates = []
        for r in range(rows):
            i = z * rows + r
            one = wr[i]
            size = cols
            while size > 8:
                size //= 2
                one = one[:size] * one[size:]
            while size > 1:
                size //= 2
                one = one * pltpu.roll(one, size, 0)
            pw[i] = one[0:1]
            rates.append(one[0:1] * swap(one)[0:1])
        for p in range(rows // 2):
            pc_msg[z * (rows // 2) + p] = jnp.where(low((1, lanes)), rates[2 * p], rates[2 * p + 1])
        return unused

    lax.fori_loop(0, ha, products, 0)
    made_pc = []
    for d in range(1, chips):
        c = lax.rem(chip + d, chips)
        made_pc.append(remote(pc_msg, pc_land.at[chip], s_pc.at[d], r_pc.at[d], across(c)))
    for c in made_pc:
        c.start()
    sends.extend(made_pc)

    lax.fori_loop(1, ha // 2 + 1, widen(n, bb), 0)

    def wide_copy(k, z, message, landing, source, to):
        return remote(
            message.at[z], landing.at[source, z], s_wide.at[k, z, to], r_wide.at[k, z, source], across(to)
        )

    def wide_send(k, z, message, landing, backward):
        for c in range(chips):

            @pl.when(c < chip if backward else c > chip)
            def _():
                wide_copy(k, z, message, landing, chip, c).start()

    def wide_done(k, z, message, landing, backward):
        for c in range(chips):

            @pl.when(c < chip if backward else c > chip)
            def _():
                wide_copy(k, z, message, landing, chip, c).wait_send()

    def wide_arrive(k, z, message, landing, backward):
        for c in range(chips):

            @pl.when(c > chip if backward else c < chip)
            def _():
                wide_copy(k, z, message, landing, c, c).wait_recv()

    def join(z, ends, message, backward):
        for p in range(rows // 2):
            i = z * rows + 2 * p
            a = ends[i] + pw[i] * swap(ends[i])
            b = ends[i + 1] + pw[i + 1] * swap(ends[i + 1])
            message[z, p] = jnp.where(keep, a, swap(b)) if backward else jnp.where(keep, swap(a), b)

    def enter(z, ends, landing, target, backward):
        def step(t, carry):
            c = chips - 1 - t if backward else t
            return tuple(
                pc_land[c, z * (rows // 2) + p] * carry[p] + landing[c, z, p] for p in range(rows // 2)
            )

        zero = jnp.zeros((n, lanes), F32)
        carry = lax.fori_loop(0, chips - 1 - chip if backward else chip, step, (zero,) * (rows // 2))
        for p in range(rows // 2):
            for s in range(2):
                i = z * rows + 2 * p + s
                k = swap(carry[p]) if (s == 0) == backward else carry[p]
                after = swap(ends[i] + pw[i] * k)
                target[i] = jnp.where(keep, after, k) if backward else jnp.where(keep, k, after)

    def col_scan(c, unused):
        z = ha - 1 - c
        gather_in(0, z, msg_c, land_c, cot)

        def one(t, unused):
            i = z * rows + rows - 1 - t
            carry = jnp.zeros((n, lanes), F32)
            for j in range(cols - 1, -1, -1):
                grad = cb[i, j] * cot[i, j : j + 1, :] + hold[j]
                grads[i, j] = grad
                hold[j] = hr[i, j : j + 1, :] * grad
                carry = wr[i, j : j + 1, :] * (grad + carry)
            ends_b[i] = carry
            return unused

        lax.fori_loop(0, rows, one, 0, unroll=True)
        join(z, ends_b, wb_msg, True)
        wide_send(0, z, wb_msg, wb_land, True)
        return unused

    lax.fori_loop(0, ha, col_scan, 0)
    lax.fori_loop(ha // 2 + 1, ha, widen(n, bb), 0)
    arrive(made_pc)

    def row_scan(c, unused):
        z = lax.rem(me_z + c, ha)
        gather_in(1, z, msg_x, land_x, x)

        def one(r, unused):
            i = z * rows + r
            carry = bb[i, 0] * x[i, 0:1, :]
            for j in range(1, cols):
                carry = wr[i, j : j + 1, :] * carry + bb[i, j] * x[i, j : j + 1, :]
            ends_f[i] = carry
            return unused

        lax.fori_loop(0, rows, one, 0, unroll=True)
        join(z, ends_f, wf_msg, False)
        wide_send(1, z, wf_msg, wf_land, False)
        return unused

    lax.fori_loop(0, ha, row_scan, 0)

    def keep_product(kept, r, j, v):
        top = v.astype(BF16)
        kept[r, 0:n, j * lanes : (j + 1) * lanes] = top
        kept[r, n:, j * lanes : (j + 1) * lanes] = (v - top.astype(F32)).astype(BF16)

    row_of = lax.div(lax.broadcasted_iota(jnp.int32, (n, tokens), 1), cols)

    def channel_sums(kept, message, z):
        v = jnp.dot(kept.reshape(rows * 2 * n, cols * lanes), place[...], preferred_element_type=F32)
        for e in range(pair):
            out = jnp.zeros((n, tokens), F32)
            for r in range(rows):
                part = v[r * 2 * n : (r + 1) * 2 * n, e * tokens : (e + 1) * tokens]
                out = jnp.where(row_of == r, part[:n] + part[n:], out)
            message[z * pair + e, 0:n] = out

    def group_sums():
        both = jnp.concatenate([part_w[...], part_h[...]], axis=0)
        top = both.astype(BF16)
        rest = (both - top.astype(F32)).astype(BF16)
        v = jnp.dot(jnp.concatenate([top, rest], axis=0), place[...], preferred_element_type=F32)
        v = v[: 2 * rows] + v[2 * rows :]
        sub = lax.broadcasted_iota(jnp.int32, (rows, tokens), 0)
        row = lax.div(lax.broadcasted_iota(jnp.int32, (rows, tokens), 1), cols)
        out = []
        for e in range(pair):
            part = v[:, e * tokens : (e + 1) * tokens]
            out.append(
                [
                    jnp.sum(jnp.where(sub == row, part[k * rows : (k + 1) * rows], 0.0), axis=0, keepdims=True)
                    for k in range(2)
                ]
            )
        return out

    def home(k, z, e, message, landing):
        q = z * pair + e
        return remote(message.at[q], landing.at[me_q], s_out.at[k, q], r_out.at[k, me_q], column(q))

    def go_home(k, z, message, landing):
        for e in range(pair):

            @pl.when(z * pair + e != me_q)
            def _():
                home(k, z, e, message, landing).start()

            @pl.when(z * pair + e == me_q)
            def _():
                pltpu.make_async_copy(message.at[me_q], landing.at[me_q], s_own.at[k]).start()

    def rows_done(c, unused):
        z = lax.rem(me_z + ha // 2 + c, ha)
        wide_arrive(0, z, wb_msg, wb_land, True)
        enter(z, ends_b, wb_land, cin_b, True)

        def one(r, unused):
            i = z * rows + r
            carry = cin_b[i]
            for j in range(cols - 1, -1, -1):
                grad = grads[i, j] + carry
                rows_grad[i, j] = grad
                carry = wr[i, j : j + 1, :] * grad
                tok_rows[r, j : j + 1, :] = jnp.sum(grad * bb[i, j], axis=0, keepdims=True)
                keep_product(prod_in, i, j, grad * x[i, j : j + 1, :])
            return unused

        lax.fori_loop(0, rows, one, 0, unroll=True)
        for r in range(rows):
            a, b = cross(tok_rows[r, 0 : cols // 2, :], tok_rows[r, cols // 2 :, :])
            tok_msg[z * pair, r] = a
            tok_msg[z * pair + 1, r] = b
        go_home(0, z, tok_msg, tok_home)
        channel_sums(prod_in[pl.ds(z * rows, rows)], in_msg, z)
        go_home(1, z, in_msg, in_home)
        return unused

    lax.fori_loop(0, ha, rows_done, 0)

    sub = lax.broadcasted_iota(jnp.int32, (8, tokens), 0)

    def cols_done(z, unused):
        wide_arrive(1, z, wf_msg, wf_land, False)
        enter(z, ends_f, wf_land, cin_f, False)

        def one(r, unused):
            i = z * rows + r
            carry = cin_f[i]
            for j in range(cols):
                w = rows_grad[i, j] * carry
                carry = wr[i, j : j + 1, :] * carry + bb[i, j] * x[i, j : j + 1, :]
                before = total[j]
                h = grads[i, j] * before
                now = hr[i, j : j + 1, :] * before + carry
                total[j] = now
                keep_product(prod, r, j, now * cot[i, j : j + 1, :])
                part_w[pl.ds(r, 1), j * lanes : (j + 1) * lanes] = jnp.sum(w, axis=0, keepdims=True)
                part_h[pl.ds(r, 1), j * lanes : (j + 1) * lanes] = jnp.sum(h, axis=0, keepdims=True)
            return unused

        lax.fori_loop(0, rows, one, 0, unroll=True)
        channel_sums(prod[...], fin_msg, z)
        for e, (w, h) in enumerate(group_sums()):
            fin_msg[z * pair + e, n:] = jnp.where(sub == 0, w, jnp.where(sub == 1, h, 0.0))
        go_home(2, z, fin_msg, fin_home)
        return unused

    lax.fori_loop(0, ha, cols_done, 0)

    for c in sends:
        c.wait_send()

    homes = ((0, tok_msg, tok_home), (1, in_msg, in_home), (2, fin_msg, fin_home))

    def sent(z, unused):
        wide_done(0, z, wb_msg, wb_land, True)
        wide_done(1, z, wf_msg, wf_land, False)
        for k, message, landing in homes:
            for e in range(pair):

                @pl.when(z * pair + e != me_q)
                def _():
                    home(k, z, e, message, landing).wait_send()

        return unused

    lax.fori_loop(0, ha, sent, 0)
    for k, message, landing in homes:
        for d in range(1, owners):
            q = lax.rem(me_q + d, owners)
            remote(message.at[q], landing.at[q], s_out.at[k, q], r_out.at[k, q], column(q)).wait_recv()
    for k, message, landing in ((0, tok_msg, tok_home), (1, in_msg, in_home), (2, fin_msg, fin_home)):
        pltpu.make_async_copy(message.at[me_q], landing.at[me_q], s_own.at[k]).wait()


def at_home(ha, pair, tok_home, in_home, fin_home, wl, hl, tok_out, in_out, so_out, wg_out, hg_out):
    rows, cols, channels = tok_out.shape
    n = in_out.shape[1]
    groups = wl.shape[1]
    lanes = channels // ha
    owners = ha * pair
    tokens = rows * cols
    for z in range(ha):
        for r in range(rows):
            a, b = cross(tok_home[z * pair, r], tok_home[z * pair + 1, r])
            tok_out[r, 0 : cols // 2, z * lanes : (z + 1) * lanes] = a
            tok_out[r, cols // 2 :, z * lanes : (z + 1) * lanes] = b
    in_sum, so_sum = in_home[0], fin_home[0, 0:n]
    for q in range(1, owners):
        in_sum = in_sum + in_home[q]
        so_sum = so_sum + fin_home[q, 0:n]
    in_out[...] = in_sum.T
    so_out[...] = so_sum.T
    sub = lax.broadcasted_iota(jnp.int32, (groups, tokens), 0)
    for k, decay, out in ((0, wl, wg_out), (1, hl, hg_out)):
        rate_sum = jnp.zeros((groups, tokens), F32)
        for q in range(owners):
            g = q * groups // owners
            rate_sum = rate_sum + jnp.where(sub == g, fin_home[q, n + k : n + k + 1, :], 0.0)
        for r in range(rows):
            out[r] = rate_sum[:, r * cols : (r + 1) * cols] * jnp.exp(decay[r])


def per_device(ha, wa, tokens, cotangent, state_in, state_out, width_decay, height_decay):
    rows, cols, channels = tokens.shape
    n = state_in.shape[2]
    groups = width_decay.shape[2]
    pair = 2
    chips = wa // pair
    owners = ha * pair
    lanes = channels // ha
    high = ha * rows
    count = rows * cols
    vmem = pl.BlockSpec(memory_space=pltpu.VMEM)
    far = pl.BlockSpec(memory_space=pl.ANY)
    room = lambda *shape: pltpu.VMEM(shape, F32)
    sems = lambda *shape: pltpu.SemaphoreType.DMA(shape)
    wl = jnp.swapaxes(width_decay, 1, 2)
    hl = jnp.swapaxes(height_decay, 1, 2)
    message = (owners, rows, cols // 2, lanes)
    state = (high, cols, n, lanes)
    ends = (high, n, lanes)
    wide = (ha, rows // 2, n, lanes)
    homes = pl.pallas_call(
        functools.partial(exchange, ha, chips, pair),
        out_shape=[
            jax.ShapeDtypeStruct(message, F32),
            jax.ShapeDtypeStruct((owners, n, count), F32),
            jax.ShapeDtypeStruct((owners, n + 8, count), F32),
        ],
        in_specs=[far] * 6,
        out_specs=[far] * 3,
        scratch_shapes=[
            pltpu.VMEM(tokens.shape, tokens.dtype),
            pltpu.VMEM(cotangent.shape, cotangent.dtype),
            room(*state_in.shape),
            room(*state_out.shape),
            room(*wl.shape),
            room(*hl.shape),
        ]
        + [room(*message) for _ in range(4)]
        + [room(pair, ha, 2 * n + 2 * groups, count)]
        + [room(high, cols, lanes) for _ in range(4)]
        + [room(*state) for _ in range(4)]
        + [room(cols, n, lanes) for _ in range(2)]
        + [room(*ends) for _ in range(4)]
        + [room(high, 1, lanes), room(high // 2, 1, lanes), room(chips, high // 2, 1, lanes)]
        + [room(*wide), room(chips, *wide), room(*wide), room(chips, *wide)]
        + [
            pltpu.VMEM((cols * lanes, pair * count), BF16),
            pltpu.VMEM((high, 2 * n, cols * lanes), BF16),
            pltpu.VMEM((rows, 2 * n, cols * lanes), BF16),
            room(rows, cols * lanes),
            room(rows, cols * lanes),
            room(rows, cols, lanes),
            room(*message),
            room(owners, n, count),
            room(owners, n + 8, count),
        ]
        + [sems(ha), sems(ha), sems(pair, ha), sems(pair, ha)]
        + [sems(2, owners), sems(2, owners), sems(chips), sems(chips)]
        + [sems(2, ha, chips), sems(2, ha, chips), sems(3, owners), sems(3, owners), sems(6), sems(3)],
        compiler_params=pltpu.CompilerParams(
            collective_id=0, has_side_effects=True, vmem_limit_bytes=56 * 1024 * 1024
        ),
        name="exchange",
    )(tokens, cotangent, state_in, state_out, wl, hl)
    result = pl.pallas_call(
        functools.partial(at_home, ha, pair),
        out_shape=[
            jax.ShapeDtypeStruct((rows, cols, channels), F32),
            jax.ShapeDtypeStruct((count, n), F32),
            jax.ShapeDtypeStruct((count, n), F32),
            jax.ShapeDtypeStruct((rows, groups, cols), F32),
            jax.ShapeDtypeStruct((rows, groups, cols), F32),
        ],
        in_specs=[vmem] * 5,
        out_specs=[vmem] * 5,
        name="at_home",
    )(*homes, wl, hl)
    return (
        result[0],
        result[1].reshape(rows, cols, n),
        result[2].reshape(rows, cols, n),
        jnp.swapaxes(result[3], 1, 2),
        jnp.swapaxes(result[4], 1, 2),
    )


def solution(mesh):
    spec = P("ha", "wa", None)
    return jax.shard_map(
        functools.partial(per_device, mesh.shape["ha"], mesh.shape["wa"]),
        mesh=mesh,
        in_specs=(spec,) * 6,
        out_specs=(spec,) * 5,
        check_vma=False,
    )
```
